32 devices in a mesh: dp: 8 (over z, x), mp: 4 (over y, core).
Axes of the slice: x: 2, y: 2, z: 4, core: 2. Of those that a mesh axis runs over, the one named last changes fastest.
Arguments:
- block_in: bfloat16 [8, 2048, 1024], P('dp', 'mp'), may hold values from -6 to 6
- segment_ids: int32 [8, 2048], P('dp', 'mp'), may hold values from 0 to 15, never falling along the last dimension, each value on 1 to 1024 neighbouring positions
- first_gain: bfloat16 [1024], P(('dp', 'mp')), may hold values from 0.5 to 1.5
- in_proj: bfloat16 [1024, 3072], P(('dp', 'mp')), may hold values from -0.1875 to 0.1875
- conv_kernel: bfloat16 [1024, 3], P(('dp', 'mp')), may hold values from -3 to 3
- out_proj: bfloat16 [1024, 1024], P(('dp', 'mp')), may hold values from -0.1875 to 0.1875
- second_gain: bfloat16 [1024], P(('dp', 'mp')), may hold values from 0.5 to 1.5
- gate_proj: bfloat16 [1024, 4608], P(None, 'mp'), may hold values from -0.1875 to 0.1875
- up_proj: bfloat16 [1024, 4608], P(None, 'mp'), may hold values from -0.1875 to 0.1875
- down_proj: bfloat16 [4608, 1024], P('mp'), may hold values from -0.125 to 0.125
- out_grad: bfloat16 [8, 2048, 1024], P('dp', 'mp'), may hold values from -6 to 6
Outputs:
- layer_out: bfloat16 [8, 2048, 1024], P('dp', 'mp')
- input_grad: float32 [8, 2048, 1024], P('dp', 'mp')
- grad_first: float32 [1024], P(('dp', 'mp'))
- grad_in: float32 [1024, 3072], P(('dp', 'mp'))
- grad_conv: float32 [1024, 3], P(('dp', 'mp'))
- grad_out: float32 [1024, 1024], P(('dp', 'mp'))
- grad_second: float32 [1024], P(('dp', 'mp'))
- grad_gate: float32 [1024, 4608], P(None, 'mp')
- grad_up: float32 [1024, 4608], P(None, 'mp')
- grad_down: float32 [4608, 1024], P('mp')
The draws below stay inside these ranges and needn't reach their ends.
Inputs may be any that keep to these rules, and one draw needn't show every extreme that they name: `segment_ids`: along each sequence the ids never fall and each document is one run of positions; the longest document has exactly 1024 tokens.
All inputs are finite; a program needn't handle non-finite values.
Results may differ from the reference program's by a relative error of at most 0.013.
Values may be sent and summed in bfloat16 or wider, within the bound.
No kernel may reach another device: no remote copies, remote signals or barrier semaphores. Data moves between devices by JAX's collectives and lax.ppermute only.
A program may use at most 192 MiB of HBM per device.

```python
import math
import jax
import jax.numpy as jnp
import numpy as np
from jax import lax

D = 1024
FF = 4608
KERNEL = 3
SEQ_LEN = 2048
SEQS = 8


def block_levels(key, shape, split, low, top_value):
    factor_of, own = 1.0, jax.random.fold_in(key, 6)
    for dim, parts in split:
        steps = jnp.exp(jax.random.uniform(jax.random.fold_in(own, dim), (parts,), jnp.float32, low / len(split), top_value / len(split)))
        factor_of = factor_of * jnp.repeat(steps, shape[dim] // parts).reshape([-1 if axis == dim else 1 for axis in range(len(shape))])
    return factor_of


def profile(number_of, total, limit, slope):
    loads = [(1 << 20) // math.isqrt(rank ** slope) + 1 for rank in range(2, number_of + 1)]
    spare, counts = total - limit - (number_of - 1), [1] * (number_of - 1)
    while spare > 0:
        free = [i for i in range(number_of - 1) if counts[i] < limit]
        mass, left = sum([loads[i] for i in free]), spare
        for i in free:
            addition = min(limit - counts[i], max(1, left * loads[i] // mass), spare)
            counts[i] = counts[i] + addition
            spare = spare - addition
    return np.array([limit] + counts)


def uneven(key, amount, total, reach, lean):
    if amount == 2:
        one = jax.random.randint(key, (), max(1, total - reach), min(reach, total - 1) + 1)
        return jnp.stack([one, total - one])
    sizes = jnp.asarray(profile(amount, total, reach, lean), jnp.int32)
    pairs = (amount - 1) // 2
    giver, taker = sizes[1:1 + 2 * pairs:2], sizes[2:2 + 2 * pairs:2]
    slack = jnp.minimum(giver - 1, reach - taker)
    shifted = jax.random.randint(jax.random.fold_in(key, 1), (pairs,), 0, 1 << 20) % (slack + 1)
    sizes = sizes.at[1:1 + 2 * pairs:2].set(giver - shifted).at[2:2 + 2 * pairs:2].set(taker + shifted)
    return sizes[jax.random.permutation(jax.random.fold_in(key, 2), amount)]


def gaussian(key, dims, width, most, shards=(), kind=jnp.bfloat16):
    result = jax.random.normal(key, dims, jnp.float32) * width
    if len(shards) > 0:
        result = block_levels(key, dims, shards, -0.22, 0.18) * result
    return jnp.clip(result, min=-most, max=most).astype(kind)


def setup_inputs(seed: int = 0) -> dict:
    key_of = jax.random.split(jax.random.key(seed), 12)
    block_in = gaussian(key_of[0], (SEQS, SEQ_LEN, D), 1.0, 6.0, ((0, 8), (1, 4)))
    segment_ids = jax.vmap(lambda own: jnp.searchsorted(jnp.cumsum(uneven(own, max(4, SEQ_LEN // 128), SEQ_LEN, SEQ_LEN // 2, 2)), jnp.arange(SEQ_LEN), side="right"))(jax.random.split(key_of[1], SEQS)).reshape((SEQS, SEQ_LEN)).astype(jnp.int32)
    first_gain = jnp.clip(1.0 + 0.1 * jax.random.normal(key_of[2], (D,), jnp.float32), 0.5, 1.5).astype(jnp.bfloat16)
    in_proj = gaussian(key_of[3], (D, 3 * D), D ** -0.5, 0.1875, ((0, 32),))
    conv_kernel = gaussian(key_of[4], (D, KERNEL), 0.6, 3.0, ((0, 32),))
    out_proj = gaussian(key_of[5], (D, D), D ** -0.5, 0.1875, ((0, 32),))
    second_gain = jnp.clip(1.0 + 0.1 * jax.random.normal(key_of[6], (D,), jnp.float32), 0.5, 1.5).astype(jnp.bfloat16)
    gate_proj = gaussian(key_of[7], (D, FF), D ** -0.5, 0.1875, ((1, 4),))
    up_proj = gaussian(key_of[8], (D, FF), D ** -0.5, 0.1875, ((1, 4),))
    down_proj = gaussian(key_of[9], (FF, D), (FF // 2) ** -0.5, 0.125, ((0, 4),))
    out_grad = gaussian(key_of[10], (SEQS, SEQ_LEN, D), 1.0, 6.0, ((0, 8), (1, 4)))
    return {"block_in": block_in, "segment_ids": segment_ids, "first_gain": first_gain, "in_proj": in_proj, "conv_kernel": conv_kernel, "out_proj": out_proj, "second_gain": second_gain, "gate_proj": gate_proj, "up_proj": up_proj, "down_proj": down_proj, "out_grad": out_grad}


epsilon = 1e-05

@jax.custom_vjp
def low(v):
    return lax.optimization_barrier(v.astype(jnp.bfloat16)).astype(jnp.float32)

@jax.custom_vjp
def low_back(v):
    return v

def low_keep(v):
    return (low(v), None)

def low_pass(kept, grad):
    return (grad,)

def back_keep(v):
    return (v, None)

def back_low(kept, grad):
    return (low(grad),)
low.defvjp(low_keep, low_pass)
low_back.defvjp(back_keep, back_low)

def rms_norm(values, scale):
    return values * lax.rsqrt(lax.optimization_barrier(jnp.mean(values * values, axis=-1, keepdims=True)) + epsilon) * scale

def matmul(left, right):
    return jnp.dot(left, right, precision=lax.Precision.HIGHEST, preferred_element_type=jnp.float32)

def causal_conv(product, segments, kernel):
    length = product.shape[0]
    padded = jnp.concatenate([jnp.zeros((KERNEL - 1, product.shape[1]), product.dtype), product], 0)
    padded_ids = jnp.concatenate([jnp.full((KERNEL - 1,), -1, jnp.int32), segments.astype(jnp.int32)], 0)
    summed = jnp.zeros_like(product)
    for offset in range(KERNEL):
        same = (padded_ids[offset:offset + length] == segments.astype(jnp.int32))[:, None]
        summed = summed + jnp.where(same, padded[offset:offset + length], 0.0) * kernel[:, offset]
    return summed

def layer_forward(segments, values, first_gain, in_proj, conv_kernel, out_proj, second_gain, gate_proj, up_proj, down_proj):
    first_low = low(rms_norm(values, first_gain))
    mixer = low_back(matmul(first_low, in_proj))
    opening = mixer[:, :D]
    closing = mixer[:, D:2 * D]
    carried = mixer[:, 2 * D:]
    gated = low(closing * causal_conv(opening * carried, segments, conv_kernel))
    residual = values + low_back(matmul(gated, out_proj))
    second_low = low(rms_norm(residual, second_gain))
    gate_val = low_back(matmul(second_low, gate_proj))
    up_val = low_back(matmul(second_low, up_proj))
    hidden = low(jax.nn.silu(gate_val) * up_val)
    return residual + low_back(matmul(hidden, down_proj))

def reference(block_in, segment_ids, first_gain, in_proj, conv_kernel, out_proj, second_gain, gate_proj, up_proj, down_proj, out_grad):
    weights = tuple((tensor.astype(jnp.float32) for tensor in (first_gain, in_proj, conv_kernel, out_proj, second_gain, gate_proj, up_proj, down_proj)))

    def one_sequence(totals, inputs):
        values, segments, cotangent = inputs

        def forward(values_in, *params):
            return layer_forward(segments, values_in, *params)
        output, pull_back = jax.vjp(forward, values.astype(jnp.float32), *weights)
        gradients = pull_back(cotangent.astype(jnp.float32))
        totals = tuple((summed + update for summed, update in zip(totals, gradients[1:])))
        return (totals, (output.astype(jnp.bfloat16), gradients[0]))
    start_sums = tuple((jnp.zeros_like(tensor) for tensor in weights))
    totals, (outputs, input_grad) = lax.scan(one_sequence, start_sums, (block_in, segment_ids, out_grad))
    return (outputs, input_grad, totals[0], totals[1], totals[2], totals[3], totals[4], totals[5], totals[6], totals[7])
```

```python
import jax
import jax.numpy as jnp
from jax import lax
from jax.sharding import PartitionSpec as P

KERNEL = 3
LANES = 128
BF16 = jnp.bfloat16
F32 = jnp.float32

epsilon = 1e-05


def swap(block, axis, bit):
    size = lax.axis_size(axis)
    return lax.ppermute(block, axis, [(i, i ^ (1 << bit)) for i in range(size)])


def shift(block, axis, distance):
    devices = range(lax.axis_size(axis))
    route = [(i - distance, i) for i in devices if i - distance in devices]
    return lax.ppermute(block, axis, route)


def bit_of(axis, bit):
    return (lax.axis_index(axis) >> bit) & 1


def bits_of(axis):
    size = lax.axis_size(axis)
    assert size & (size - 1) == 0
    return size.bit_length() - 1


def inner_rows(left, right):
    return lax.dot_general(
        left, right, (((0,), (0,)), ((), ())), preferred_element_type=F32
    )


def inner_cols(left, right):
    return lax.dot_general(
        left, right, (((1,), (1,)), ((), ())), preferred_element_type=F32
    )


def add_low(one, two):
    return (one.astype(F32) + two.astype(F32)).astype(BF16)


def gather_mp(own):
    blocks = [own]
    for bit in reversed(range(bits_of("mp"))):
        blocks = blocks + [None] * len(blocks)
    size = lax.axis_size("mp")
    blocks = [own] + [None] * (size - 1)
    for bit in reversed(range(bits_of("mp"))):
        have = [r for r in range(size) if blocks[r] is not None]
        for r in have:
            blocks[r ^ (1 << bit)] = swap(blocks[r], "mp", bit)
    return blocks


def scatter_mp(blocks):
    held = {r: block for r, block in enumerate(blocks)}
    for bit in range(bits_of("mp")):
        sent = [r for r in held if r >> bit & 1]
        kept = [r for r in held if not r >> bit & 1]
        got = swap(jnp.concatenate([held[r] for r in sent], 0), "mp", bit)
        rows = got.shape[0] // len(sent)
        for n, r in enumerate(sent):
            there = r ^ (1 << bit)
            held[there] = held[there].astype(F32) + got[n * rows : (n + 1) * rows].astype(F32)
        final = bit == bits_of("mp") - 1
        held = {r: held[r] if final else held[r].astype(BF16) for r in kept}
    return held[0]


def sum_dp(array):
    count = bits_of("dp")
    halved = list(range(min(count, 3)))
    for bit in halved:
        half = array.shape[0] // 2
        mine = bit_of("dp", bit)
        sent = lax.dynamic_slice_in_dim(array, (1 - mine) * half, half, 0)
        kept = lax.dynamic_slice_in_dim(array, mine * half, half, 0)
        array = add_low(kept, swap(sent, "dp", bit))
    for bit in range(len(halved), count):
        array = add_low(array, swap(array, "dp", bit))
    for bit in reversed(halved):
        got = swap(array, "dp", bit)
        low_first = bit_of("dp", bit) == 0
        array = jnp.concatenate(
            [jnp.where(low_first, array, got), jnp.where(low_first, got, array)], 0
        )
    return array


def scatter_all(array):
    steps = [("mp", b) for b in range(bits_of("mp"))] + [("dp", b) for b in range(bits_of("dp"))]
    count = len(steps)
    rows = array.shape[0] >> count
    array = array.reshape(array.shape[0] // rows, rows, array.shape[1])
    for axis, bit in steps:
        pairs = array.reshape(array.shape[0] // 2, 2, rows, array.shape[2])
        mine = bit_of(axis, bit)
        sent = lax.dynamic_index_in_dim(pairs, 1 - mine, 1, keepdims=False)
        kept = lax.dynamic_index_in_dim(pairs, mine, 1, keepdims=False)
        array = add_low(kept, swap(sent, axis, bit))
    return array[0]


def per_device(
    block_in,
    segment_ids,
    first_gain,
    in_proj,
    conv_kernel,
    out_proj,
    second_gain,
    gate_proj,
    up_proj,
    down_proj,
    out_grad,
):
    rows = block_in.shape[1]
    features = block_in.shape[2]
    lookback = KERNEL - 1
    x = block_in.reshape(rows, features).astype(F32)
    own_ids = segment_ids.reshape(rows)
    cotangent = out_grad.reshape(rows, features)

    small = jnp.concatenate(
        [first_gain[:, None], second_gain[:, None], conv_kernel], 1
    )
    small = jnp.pad(small, ((0, 0), (0, LANES - small.shape[1])))
    packed = jnp.concatenate([in_proj, out_proj, small], 1)
    everything = lax.all_gather(packed, ("dp", "mp"), axis=0, tiled=True)
    weight_in = everything[:, : 3 * features]
    weight_out = everything[:, 3 * features : 4 * features]
    vectors = everything[:, 4 * features : 4 * features + 2 + KERNEL].astype(F32).T
    gain_one, gain_two, taps = vectors[0], vectors[1], vectors[2:]

    group_grad = gather_mp(cotangent)

    inverse_one = lax.rsqrt(jnp.mean(x * x, axis=-1, keepdims=True) + epsilon)
    unit_one = x * inverse_one
    first_low = (unit_one * gain_one).astype(BF16)
    mixer = jnp.dot(first_low, weight_in, preferred_element_type=F32)
    opening = mixer[:, :features]
    closing = mixer[:, features : 2 * features]
    carried = mixer[:, 2 * features :]
    product = opening * carried
    rim_rows = shift(product[rows - lookback :], "mp", 1)
    rim_ids = shift(own_ids[rows - lookback :].astype(F32), "mp", 1).astype(jnp.int32)
    first = lax.axis_index("mp") == 0
    rim_ids = jnp.where(first, -1, rim_ids)
    extended = jnp.concatenate([rim_rows, product], 0)
    extended_ids = jnp.concatenate([rim_ids, own_ids], 0)
    same = [
        (extended_ids[k : k + rows] == own_ids)[:, None] for k in range(KERNEL)
    ]
    past = [jnp.where(same[k], extended[k : k + rows], 0.0) for k in range(KERNEL)]
    conv = sum(past[k] * taps[k] for k in range(KERNEL))
    gated_low = (closing * conv).astype(BF16)
    residual = x + jnp.dot(gated_low, weight_out, preferred_element_type=F32)
    inverse_two = lax.rsqrt(jnp.mean(residual * residual, axis=-1, keepdims=True) + epsilon)
    second_low = (residual * inverse_two * gain_two).astype(BF16)

    group = jnp.concatenate(gather_mp(second_low), 0)
    grads = jnp.concatenate(group_grad, 0)
    gate_val = jnp.dot(group, gate_proj, preferred_element_type=F32)
    up_val = jnp.dot(group, up_proj, preferred_element_type=F32)
    sig = jax.nn.sigmoid(gate_val)
    silu = gate_val * sig
    hidden = (silu * up_val).astype(BF16)
    down_local = inner_rows(hidden, grads).astype(BF16)
    grad_down = sum_dp(down_local).astype(F32)
    hidden_grad = inner_cols(grads, down_proj)
    gate_low = (hidden_grad * up_val * sig * (1 + gate_val * (1 - sig))).astype(BF16)
    up_low = (hidden_grad * silu).astype(BF16)
    second_parts = (inner_cols(gate_low, gate_proj) + inner_cols(up_low, up_proj)).astype(BF16)
    size = lax.axis_size("mp")
    second_grad = scatter_mp([second_parts[r * rows : (r + 1) * rows] for r in range(size)])
    grad_gate = sum_dp(inner_rows(group, gate_low).astype(BF16)).astype(F32)
    grad_up = sum_dp(inner_rows(group, up_low).astype(BF16)).astype(F32)
    branch_parts = jnp.dot(hidden, down_proj, preferred_element_type=F32).astype(BF16)
    branch = scatter_mp([branch_parts[r * rows : (r + 1) * rows] for r in range(size)])
    layer_out = (residual + branch).astype(BF16).reshape(1, rows, features)

    unit_two = residual * inverse_two
    weighted = second_grad * gain_two
    residual_grad = cotangent.astype(F32) + inverse_two * (
        weighted - unit_two * jnp.mean(weighted * unit_two, axis=-1, keepdims=True)
    )
    second_local = jnp.sum(second_grad * unit_two, axis=0)
    residual_low = residual_grad.astype(BF16)
    out_local = inner_rows(gated_low, residual_low)
    gated_grad = inner_cols(residual_low, weight_out)
    closing_grad = gated_grad * conv
    conv_grad = gated_grad * closing
    kernel_local = [jnp.sum(conv_grad * past[k], axis=0) for k in range(KERNEL)]
    spread = jnp.zeros((rows + lookback, features), F32)
    spread = sum(
        jnp.pad(jnp.where(same[k], conv_grad * taps[k], 0.0), ((k, lookback - k), (0, 0)))
        for k in range(KERNEL)
    )
    rim_back = shift(spread[:lookback], "mp", -1)
    product_grad = spread[lookback:] + jnp.pad(rim_back, ((rows - lookback, 0), (0, 0)))
    mixer_grad = jnp.concatenate(
        [product_grad * carried, closing_grad, product_grad * opening], 1
    ).astype(BF16)
    in_local = inner_rows(first_low, mixer_grad).astype(BF16)
    first_grad = inner_cols(mixer_grad, weight_in)
    weighted = first_grad * gain_one
    input_grad = residual_grad + inverse_one * (
        weighted - unit_one * jnp.mean(weighted * unit_one, axis=-1, keepdims=True)
    )
    input_grad = input_grad.reshape(1, rows, features)

    small_local = jnp.stack([second_local] + kernel_local, 1).astype(BF16)
    small_local = jnp.pad(small_local, ((0, 0), (0, LANES - small_local.shape[1])))
    early = scatter_all(jnp.concatenate([out_local.astype(BF16), small_local], 1)).astype(F32)
    grad_out = early[:, :features]
    grad_second = early[:, features]
    grad_conv = early[:, features + 1 : features + 1 + KERNEL]
    grad_in = scatter_all(in_local).astype(F32)
    grad_first = jnp.sum(grad_in * in_proj.astype(F32), axis=1) / first_gain.astype(F32)
    return (
        layer_out,
        input_grad,
        grad_first,
        grad_in,
        grad_conv,
        grad_out,
        grad_second,
        grad_gate,
        grad_up,
        grad_down,
    )


def solution(mesh):
    in_specs = (
        P("dp", "mp", None),
        P("dp", "mp"),
        P(("dp", "mp")),
        P(("dp", "mp"), None),
        P(("dp", "mp"), None),
        P(("dp", "mp"), None),
        P(("dp", "mp")),
        P(None, "mp"),
        P(None, "mp"),
        P("mp", None),
        P("dp", "mp", None),
    )
    out_specs = (
        P("dp", "mp", None),
        P("dp", "mp", None),
        P(("dp", "mp")),
        P(("dp", "mp"), None),
        P(("dp", "mp"), None),
        P(("dp", "mp"), None),
        P(("dp", "mp")),
        P(None, "mp"),
        P(None, "mp"),
        P("mp", None),
    )
    return jax.shard_map(
        per_device, mesh=mesh, in_specs=in_specs, out_specs=out_specs, check_vma=False
    )
```

```python
import jax
import jax.numpy as jnp
from jax import lax
from jax.experimental import pallas as pl
from jax.experimental.pallas import tpu as pltpu
from jax.sharding import PartitionSpec as P

KERNEL = 3
LANES = 128
BF16 = jnp.bfloat16
F32 = jnp.float32
HALVINGS = 3
PARTS = 1 << HALVINGS
ORDER = [int(format(q, "03b")[::-1], 2) for q in range(PARTS)]
NN = (((1,), (0,)), ((), ()))
NT = (((1,), (1,)), ((), ()))
TN = (((0,), (0,)), ((), ()))
VMEM_LIMIT = 60 * 1024 * 1024

epsilon = 1e-05


def swap(block, axis, bit):
    size = lax.axis_size(axis)
    return lax.ppermute(block, axis, [(i, i ^ (1 << bit)) for i in range(size)])


def shift(block, axis, distance):
    devices = range(lax.axis_size(axis))
    route = [(i - distance, i) for i in devices if i - distance in devices]
    return lax.ppermute(block, axis, route)


def bit_of(axis, bit):
    return (lax.axis_index(axis) >> bit) & 1


def bits_of(axis):
    size = lax.axis_size(axis)
    assert size & (size - 1) == 0
    return size.bit_length() - 1


def dot(left, right, dims):
    return lax.dot_general(left, right, dims, preferred_element_type=F32)


def inner_rows(left, right):
    return dot(left, right, TN)


def inner_cols(left, right):
    return dot(left, right, NT)


def hidden_blocks(hidden):
    wide = [(256, n) for n in range(hidden // 256)]
    rest = hidden % 256
    assert rest in (0, 128)
    return wide + ([(128, hidden // 128 - 1)] if rest else [])


def feed(x_ref, go_ref, gate_ref, up_ref, down_ref, hid_ref, gl_ref, ul_ref):
    tokens = x_ref.shape[0]
    step = min(tokens, 512)
    for start in range(0, tokens, step):
        part = slice(start, start + step)
        gate_val = dot(x_ref[part], gate_ref[...], NN)
        up_val = dot(x_ref[part], up_ref[...], NN)
        hidden_grad = dot(go_ref[part], down_ref[...], NT)
        sig = 1.0 / (1.0 + jnp.exp(-gate_val))
        silu = gate_val * sig
        hid_ref[part] = (silu * up_val).astype(BF16)
        gl_ref[part] = (hidden_grad * up_val * (sig * (1.0 + gate_val * (1.0 - sig)))).astype(BF16)
        ul_ref[part] = (hidden_grad * silu).astype(BF16)


def join(first, xa_ref, xb_ref, ga_ref, gb_ref, x_ref, go_ref):
    rows = xa_ref.shape[0]

    @pl.when(first)
    def _():
        x_ref[:rows] = xa_ref[...]
        x_ref[rows:] = xb_ref[...]
        go_ref[:rows] = ga_ref[...]
        go_ref[rows:] = gb_ref[...]


def near_kernel(xa_ref, xb_ref, ga_ref, gb_ref, gate_ref, up_ref, down_ref,
                hid_ref, gl_ref, ul_ref, og_ref, ou_ref, od_ref, x_ref, go_ref):
    join(pl.program_id(0) == 0, xa_ref, xb_ref, ga_ref, gb_ref, x_ref, go_ref)
    feed(x_ref, go_ref, gate_ref, up_ref, down_ref, hid_ref, gl_ref, ul_ref)
    og_ref[...] = dot(x_ref[...], gl_ref[...], TN)
    ou_ref[...] = dot(x_ref[...], ul_ref[...], TN)
    od_ref[...] = dot(hid_ref[...], go_ref[...], TN)


def near_feed(xs, gos, gate, up, down):
    rows, features = xs[0].shape
    hidden = gate.shape[1]
    wide = 256
    tokens = 2 * rows
    whole = pl.BlockSpec((rows, features), lambda i: (0, 0), pipeline_mode=pl.Buffered(1))
    col = pl.BlockSpec((features, wide), lambda i: (0, i))
    row = pl.BlockSpec((wide, features), lambda i: (i, 0))
    act = pl.BlockSpec((tokens, wide), lambda i: (0, i))
    return pl.pallas_call(
        near_kernel,
        grid=(pl.cdiv(hidden, wide),),
        in_specs=[whole] * 4 + [col, col, row],
        out_specs=[act] * 3 + [col, col, row],
        out_shape=[jax.ShapeDtypeStruct((tokens, hidden), BF16)] * 3
        + [jax.ShapeDtypeStruct((features, hidden), F32)] * 2
        + [jax.ShapeDtypeStruct((hidden, features), F32)],
        scratch_shapes=[pltpu.VMEM((tokens, features), BF16)] * 2,
        compiler_params=pltpu.CompilerParams(vmem_limit_bytes=VMEM_LIMIT),
        cost_estimate=pl.CostEstimate(
            flops=12 * tokens * features * hidden,
            transcendentals=tokens * hidden,
            bytes_accessed=18 * features * hidden + 6 * tokens * hidden + 4 * tokens * features,
        ),
        name="near_feed",
    )(*xs, *gos, gate, up, down)


def far_kernel(place_ref, xa_ref, xb_ref, ga_ref, gb_ref, gate_ref, up_ref, down_ref,
               ng_ref, nu_ref, nd_ref, hid_ref, gl_ref, ul_ref, kept_ref, sent_ref,
               x_ref, go_ref, tg_ref, tu_ref, td_ref):
    join(pl.program_id(0) == 0, xa_ref, xb_ref, ga_ref, gb_ref, x_ref, go_ref)
    feed(x_ref, go_ref, gate_ref, up_ref, down_ref, hid_ref, gl_ref, ul_ref)
    tg_ref[...] = ng_ref[...] + dot(x_ref[...], gl_ref[...], TN)
    tu_ref[...] = nu_ref[...] + dot(x_ref[...], ul_ref[...], TN)
    td_ref[...] = nd_ref[...] + dot(hid_ref[...], go_ref[...], TN)
    features, wide = tg_ref.shape
    tall, low = features // PARTS, wide // PARTS
    for q in range(PARTS):
        part = place_ref[0] ^ ORDER[q]
        out = kept_ref.at[q] if q < PARTS // 2 else sent_ref.at[q - PARTS // 2]
        rows = pl.ds(pl.multiple_of(part * tall, tall), tall)
        at = 0
        for grad_ref in (tg_ref, tu_ref):
            for c in range(0, wide, LANES):
                out[at : at + tall] = grad_ref[rows, c : c + LANES].astype(BF16)
                at += tall
        rows = pl.ds(pl.multiple_of(part * low, low), low)
        for c in range(0, features, LANES):
            out[at : at + low] = td_ref[rows, c : c + LANES].astype(BF16)
            at += low


def far_feed(place, xs, gos, gate, up, down, near_grads, wide, index):
    rows, features = xs[0].shape
    tokens = 2 * rows
    whole = pl.BlockSpec((rows, features), lambda i, _: (0, 0), pipeline_mode=pl.Buffered(1))
    col = pl.BlockSpec((features, wide), lambda i, _: (0, index))
    row = pl.BlockSpec((wide, features), lambda i, _: (index, 0))
    act = pl.BlockSpec((tokens, wide), lambda i, _: (0, 0))
    packed = 3 * features * wide // PARTS // LANES
    half = pl.BlockSpec((PARTS // 2, packed, LANES), lambda i, _: (0, 0, 0))
    return pl.pallas_call(
        far_kernel,
        grid_spec=pltpu.PrefetchScalarGridSpec(
            num_scalar_prefetch=1,
            grid=(1,),
            in_specs=[whole] * 4 + [col, col, row] + [col, col, row],
            out_specs=[act] * 3 + [half] * 2,
            scratch_shapes=[pltpu.VMEM((tokens, features), BF16)] * 2
            + [pltpu.VMEM((features, wide), F32)] * 2
            + [pltpu.VMEM((wide, features), F32)],
        ),
        out_shape=[jax.ShapeDtypeStruct((tokens, wide), BF16)] * 3
        + [jax.ShapeDtypeStruct((PARTS // 2, packed, LANES), BF16)] * 2,
        compiler_params=pltpu.CompilerParams(vmem_limit_bytes=VMEM_LIMIT),
        cost_estimate=pl.CostEstimate(
            flops=12 * tokens * features * wide,
            transcendentals=tokens * wide,
            bytes_accessed=24 * features * wide + 6 * tokens * wide + 4 * tokens * features,
        ),
        name="far_feed",
    )(place, *xs, *gos, gate, up, down, *near_grads)


def unpack_kernel(place_ref, own_ref, two_ref, four_ref, eight_ref, *refs):
    og_ref, ou_ref, od_ref = refs[-3:]
    features, wide = og_ref.shape
    tall, low = features // PARTS, wide // PARTS
    sources = [own_ref.at[0], two_ref.at[0]]
    sources += [four_ref.at[n] for n in range(2)]
    sources += [eight_ref.at[n] for n in range(4)]
    for q in range(PARTS):
        part = place_ref[0] ^ ORDER[q]
        source = sources[q]
        rows = pl.ds(pl.multiple_of(part * tall, tall), tall)
        at = 0
        for out in (og_ref, ou_ref):
            for c in range(0, wide, LANES):
                out[rows, c : c + LANES] = source[at : at + tall].astype(F32)
                at += tall
        rows = pl.ds(pl.multiple_of(part * low, low), low)
        for c in range(0, features, LANES):
            od_ref[rows, c : c + LANES] = source[at : at + low].astype(F32)
            at += low


def unpack(place, pieces, before, wide, index, features, hidden):
    packed = pieces[0].shape[1]
    ins = [
        pl.BlockSpec((piece.shape[0], packed, LANES), lambda i, _: (0, 0, 0)) for piece in pieces
    ]
    col = pl.BlockSpec((features, wide), lambda i, _: (0, index))
    row = pl.BlockSpec((wide, features), lambda i, _: (index, 0))
    keep = [pl.BlockSpec(memory_space=pl.ANY)] * len(before)
    return pl.pallas_call(
        unpack_kernel,
        grid_spec=pltpu.PrefetchScalarGridSpec(
            num_scalar_prefetch=1,
            grid=(1,),
            in_specs=ins + keep,
            out_specs=[col, col, row],
        ),
        out_shape=[jax.ShapeDtypeStruct((features, hidden), F32)] * 2
        + [jax.ShapeDtypeStruct((hidden, features), F32)],
        input_output_aliases={1 + len(ins) + n: n for n in range(len(before))},
        compiler_params=pltpu.CompilerParams(vmem_limit_bytes=VMEM_LIMIT),
        cost_estimate=pl.CostEstimate(
            flops=0, transcendentals=0, bytes_accessed=18 * features * wide
        ),
        name="unpack",
    )(place, *pieces, *before)


def add_low(one, two):
    return (one.astype(F32) + two.astype(F32)).astype(BF16)


def gather_mp(own):
    size = lax.axis_size("mp")
    blocks = [own] + [None] * (size - 1)
    for bit in reversed(range(bits_of("mp"))):
        for r in [r for r in range(size) if blocks[r] is not None]:
            blocks[r ^ (1 << bit)] = swap(blocks[r], "mp", bit)
    return blocks


def scatter_mp(near, far):
    rows = near.shape[0] // 2
    got_far = swap(far[rows:], "mp", 0)
    got_near = swap(near[rows:], "mp", 0)
    got = swap(add_low(far[:rows], got_far), "mp", 1)
    return near[:rows].astype(F32) + got_near.astype(F32) + got.astype(F32)


def sum_dp(kept, sent):
    for bit in range(HALVINGS):
        got = swap(sent, "dp", bit)
        half = kept.shape[0] // 2
        if half:
            sent = add_low(kept[half:], got[half:])
            kept = add_low(kept[:half], got[:half])
        else:
            kept = add_low(kept, got)
    for bit in range(HALVINGS, bits_of("dp")):
        kept = add_low(kept, swap(kept, "dp", bit))
    pieces = [kept]
    for bit in reversed(range(HALVINGS)):
        held = jnp.concatenate(pieces, 0) if len(pieces) > 1 else pieces[0]
        pieces = pieces + [swap(held, "dp", bit)]
    return pieces


def scatter_all(array):
    steps = [("mp", b) for b in range(bits_of("mp"))] + [("dp", b) for b in range(bits_of("dp"))]
    count = len(steps)
    rows = array.shape[0] >> count
    array = array.reshape(array.shape[0] // rows, rows, array.shape[1])
    for axis, bit in steps:
        pairs = array.reshape(array.shape[0] // 2, 2, rows, array.shape[2])
        mine = bit_of(axis, bit)
        sent = lax.dynamic_index_in_dim(pairs, 1 - mine, 1, keepdims=False)
        kept = lax.dynamic_index_in_dim(pairs, mine, 1, keepdims=False)
        array = add_low(kept, swap(sent, axis, bit))
    return array[0]


def per_device(
    block_in,
    segment_ids,
    first_gain,
    in_proj,
    conv_kernel,
    out_proj,
    second_gain,
    gate_proj,
    up_proj,
    down_proj,
    out_grad,
):
    rows = block_in.shape[1]
    features = block_in.shape[2]
    lookback = KERNEL - 1
    x = block_in.reshape(rows, features).astype(F32)
    own_ids = segment_ids.reshape(rows)
    cotangent = out_grad.reshape(rows, features)

    small = jnp.concatenate(
        [first_gain[:, None], second_gain[:, None], conv_kernel], 1
    )
    small = jnp.pad(small, ((0, 0), (0, LANES - small.shape[1])))
    packed = jnp.concatenate([in_proj, out_proj, small], 1)
    everything = lax.all_gather(packed, ("dp", "mp"), axis=0, tiled=True)
    weight_in = everything[:, : 3 * features]
    weight_out = everything[:, 3 * features : 4 * features]
    vectors = everything[:, 4 * features : 4 * features + 2 + KERNEL].astype(F32).T
    gain_one, gain_two, taps = vectors[0], vectors[1], vectors[2:]

    group_grad = gather_mp(cotangent)

    pad = 8
    rim = shift(block_in.reshape(rows, features)[rows - pad :], "mp", 1)
    rim_ids = shift(own_ids[rows - pad :].astype(F32), "mp", 1).astype(jnp.int32)
    rim_ids = jnp.where(lax.axis_index("mp") == 0, -1, rim_ids)
    x_all = jnp.concatenate([rim.astype(F32), x], 0)
    inverse_all = lax.rsqrt(jnp.mean(x_all * x_all, axis=-1, keepdims=True) + epsilon)
    low_all = (x_all * inverse_all * gain_one).astype(BF16)
    mixer_all = jnp.dot(low_all, weight_in, preferred_element_type=F32)
    extended = mixer_all[:, :features] * mixer_all[:, 2 * features :]
    inverse_one = inverse_all[pad:]
    unit_one = x * inverse_one
    first_low = low_all[pad:]
    mixer = mixer_all[pad:]
    opening = mixer[:, :features]
    closing = mixer[:, features : 2 * features]
    carried = mixer[:, 2 * features :]
    extended_ids = jnp.concatenate([rim_ids, own_ids], 0)
    skip = pad - lookback
    same = [
        (extended_ids[skip + k : skip + k + rows] == own_ids)[:, None] for k in range(KERNEL)
    ]
    past = [
        jnp.where(same[k], extended[skip + k : skip + k + rows], 0.0) for k in range(KERNEL)
    ]
    conv = sum(past[k] * taps[k] for k in range(KERNEL))
    gated_low = (closing * conv).astype(BF16)
    residual = x + jnp.dot(gated_low, weight_out, preferred_element_type=F32)
    inverse_two = lax.rsqrt(jnp.mean(residual * residual, axis=-1, keepdims=True) + epsilon)
    second_low = (residual * inverse_two * gain_two).astype(BF16)

    group = gather_mp(second_low)
    hidden_units = gate_proj.shape[1]
    place = (lax.axis_index("dp") % PARTS).reshape(1).astype(jnp.int32)
    hid_near, gl_near, ul_near, *near_grads = near_feed(
        group[:2], group_grad[:2], gate_proj, up_proj, down_proj
    )
    blocks = hidden_blocks(hidden_units)
    far_parts, packed = [], []
    for wide, index in blocks:
        *acts, kept, sent = far_feed(
            place, group[2:], group_grad[2:], gate_proj, up_proj, down_proj, near_grads, wide, index
        )
        far_parts.append(acts)
        packed.append((kept, sent))
    hid_far, gl_far, ul_far = (jnp.concatenate(parts, 1) for parts in zip(*far_parts))

    def back(gate_low, up_low):
        return (inner_cols(gate_low, gate_proj) + inner_cols(up_low, up_proj)).astype(BF16)

    def onward(hid):
        return dot(hid, down_proj, NN).astype(BF16)

    second_grad = scatter_mp(back(gl_near, ul_near), back(gl_far, ul_far))
    branch = scatter_mp(onward(hid_near), onward(hid_far))
    done = ()
    for (wide, index), (kept, sent) in zip(blocks, packed):
        done = unpack(place, sum_dp(kept, sent), done, wide, index, features, hidden_units)
    grad_gate, grad_up, grad_down = done
    layer_out = (residual + branch).astype(BF16).reshape(1, rows, features)

    unit_two = residual * inverse_two
    weighted = second_grad * gain_two
    residual_grad = cotangent.astype(F32) + inverse_two * (
        weighted - unit_two * jnp.mean(weighted * unit_two, axis=-1, keepdims=True)
    )
    second_local = jnp.sum(second_grad * unit_two, axis=0)
    residual_low = residual_grad.astype(BF16)
    out_local = inner_rows(gated_low, residual_low)
    gated_grad = inner_cols(residual_low, weight_out)
    closing_grad = gated_grad * conv
    conv_grad = gated_grad * closing
    kernel_local = [jnp.sum(conv_grad * past[k], axis=0) for k in range(KERNEL)]
    spread = jnp.zeros((rows + lookback, features), F32)
    spread = sum(
        jnp.pad(jnp.where(same[k], conv_grad * taps[k], 0.0), ((k, lookback - k), (0, 0)))
        for k in range(KERNEL)
    )
    rim_back = shift(spread[:lookback], "mp", -1)
    product_grad = spread[lookback:] + jnp.pad(rim_back, ((rows - lookback, 0), (0, 0)))
    mixer_grad = jnp.concatenate(
        [product_grad * carried, closing_grad, product_grad * opening], 1
    ).astype(BF16)
    in_local = inner_rows(first_low, mixer_grad).astype(BF16)
    first_grad = inner_cols(mixer_grad, weight_in)
    weighted = first_grad * gain_one
    input_grad = residual_grad + inverse_one * (
        weighted - unit_one * jnp.mean(weighted * unit_one, axis=-1, keepdims=True)
    )
    input_grad = input_grad.reshape(1, rows, features)

    small_local = jnp.stack([second_local] + kernel_local, 1).astype(BF16)
    small_local = jnp.pad(small_local, ((0, 0), (0, LANES - small_local.shape[1])))
    early = scatter_all(jnp.concatenate([out_local.astype(BF16), small_local], 1)).astype(F32)
    grad_out = early[:, :features]
    grad_second = early[:, features]
    grad_conv = early[:, features + 1 : features + 1 + KERNEL]
    grad_in = scatter_all(in_local).astype(F32)
    grad_first = jnp.sum(grad_in * in_proj.astype(F32), axis=1) / first_gain.astype(F32)
    return (
        layer_out,
        input_grad,
        grad_first,
        grad_in,
        grad_conv,
        grad_out,
        grad_second,
        grad_gate,
        grad_up,
        grad_down,
    )


def solution(mesh):
    in_specs = (
        P("dp", "mp", None),
        P("dp", "mp"),
        P(("dp", "mp")),
        P(("dp", "mp"), None),
        P(("dp", "mp"), None),
        P(("dp", "mp"), None),
        P(("dp", "mp")),
        P(None, "mp"),
        P(None, "mp"),
        P("mp", None),
        P("dp", "mp", None),
    )
    out_specs = (
        P("dp", "mp", None),
        P("dp", "mp", None),
        P(("dp", "mp")),
        P(("dp", "mp"), None),
        P(("dp", "mp"), None),
        P(("dp", "mp"), None),
        P(("dp", "mp")),
        P(None, "mp"),
        P(None, "mp"),
        P("mp", None),
    )
    return jax.shard_map(
        per_device, mesh=mesh, in_specs=in_specs, out_specs=out_specs, check_vma=False
    )
```

```python
import functools

import jax
import jax.numpy as jnp
from jax import lax
from jax.experimental import pallas as pl
from jax.experimental.pallas import tpu as pltpu
from jax.sharding import PartitionSpec as P

KERNEL = 3
LANES = 128
BF16 = jnp.bfloat16
F32 = jnp.float32
HALVINGS = 3
PARTS = 1 << HALVINGS
NN = (((1,), (0,)), ((), ()))
NT = (((1,), (1,)), ((), ()))
TN = (((0,), (0,)), ((), ()))
VMEM_LIMIT = 60 * 1024 * 1024

epsilon = 1e-05


def swap(block, axis, bit):
    size = lax.axis_size(axis)
    return lax.ppermute(block, axis, [(i, i ^ (1 << bit)) for i in range(size)])


def shift(block, axis, distance):
    devices = range(lax.axis_size(axis))
    route = [(i - distance, i) for i in devices if i - distance in devices]
    return lax.ppermute(block, axis, route)


def bit_of(axis, bit):
    return (lax.axis_index(axis) >> bit) & 1


def bits_of(axis):
    size = lax.axis_size(axis)
    assert size & (size - 1) == 0
    return size.bit_length() - 1


def after(values, *before):
    return lax.optimization_barrier((values, before))[0]


def away(bits):
    top = len(bits) - 1
    return [sum(((q >> (top - n)) & 1) << bit for n, bit in enumerate(bits)) for q in range(PARTS)]


def dot(left, right, dims):
    return lax.dot_general(left, right, dims, preferred_element_type=F32)


def inner_rows(left, right):
    return dot(left, right, TN)


def inner_cols(left, right):
    return dot(left, right, NT)


def activate(gate_val, up_val, hidden_grad):
    sig = 1.0 / (1.0 + jnp.exp(-gate_val))
    silu = gate_val * sig
    return (
        (silu * up_val).astype(BF16),
        (hidden_grad * up_val * (sig * (1.0 + gate_val * (1.0 - sig)))).astype(BF16),
        (hidden_grad * silu).astype(BF16),
    )


def feed(x_ref, go_ref, gate_ref, up_ref, down_ref, hid_ref, gl_ref, ul_ref):
    tokens = x_ref.shape[0]
    step = min(tokens, 512)
    for start in range(0, tokens, step):
        part = slice(start, start + step)
        gate_val = dot(x_ref[part], gate_ref[...], NN)
        up_val = dot(x_ref[part], up_ref[...], NN)
        hidden_grad = dot(go_ref[part], down_ref[...], NT)
        hid_ref[part], gl_ref[part], ul_ref[part] = activate(gate_val, up_val, hidden_grad)


def join(first, xa_ref, xb_ref, ga_ref, gb_ref, x_ref, go_ref):
    rows = xa_ref.shape[0]

    @pl.when(first)
    def _():
        x_ref[:rows] = xa_ref[...]
        x_ref[rows:] = xb_ref[...]
        go_ref[:rows] = ga_ref[...]
        go_ref[rows:] = gb_ref[...]


def near_kernel(xa_ref, xb_ref, ga_ref, gb_ref, gate_ref, up_ref, down_ref,
                hid_ref, gl_ref, ul_ref, og_ref, ou_ref, od_ref, x_ref, go_ref):
    join(pl.program_id(0) == 0, xa_ref, xb_ref, ga_ref, gb_ref, x_ref, go_ref)
    feed(x_ref, go_ref, gate_ref, up_ref, down_ref, hid_ref, gl_ref, ul_ref)
    og_ref[...] = dot(x_ref[...], gl_ref[...], TN).astype(BF16)
    ou_ref[...] = dot(x_ref[...], ul_ref[...], TN).astype(BF16)
    od_ref[...] = dot(hid_ref[...], go_ref[...], TN).astype(BF16)


def near_feed(xs, gos, gate, up, down):
    rows, features = xs[0].shape
    hidden = gate.shape[1]
    wide = 256
    tokens = 2 * rows
    whole = pl.BlockSpec((rows, features), lambda i: (0, 0), pipeline_mode=pl.Buffered(1))
    col = pl.BlockSpec((features, wide), lambda i: (0, i))
    row = pl.BlockSpec((wide, features), lambda i: (i, 0))
    act = pl.BlockSpec((tokens, wide), lambda i: (0, i))
    return pl.pallas_call(
        near_kernel,
        grid=(pl.cdiv(hidden, wide),),
        in_specs=[whole] * 4 + [col, col, row],
        out_specs=[act] * 3 + [col, col, row],
        out_shape=[jax.ShapeDtypeStruct((tokens, hidden), BF16)] * 3
        + [jax.ShapeDtypeStruct((features, hidden), BF16)] * 2
        + [jax.ShapeDtypeStruct((hidden, features), BF16)],
        scratch_shapes=[pltpu.VMEM((tokens, features), BF16)] * 2,
        compiler_params=pltpu.CompilerParams(vmem_limit_bytes=VMEM_LIMIT),
        cost_estimate=pl.CostEstimate(
            flops=12 * tokens * features * hidden,
            transcendentals=0,
            bytes_accessed=14 * features * hidden,
        ),
        name="near_feed",
    )(*xs, *gos, gate, up, down)


def far_kernel(orders, place_ref, xa_ref, xb_ref, ga_ref, gb_ref, gate_ref, up_ref, down_ref,
               ng_ref, nu_ref, nd_ref, *refs):
    blocks = len(orders)
    x_ref, go_ref, tg_ref, tu_ref, td_ref = refs[-5:]
    packs = refs[-5 - 2 * blocks : -5]
    hid_ref, gl_ref, ul_ref = refs[-8 - 2 * blocks : -5 - 2 * blocks]
    now = pl.program_id(0)
    join(now == 0, xa_ref, xb_ref, ga_ref, gb_ref, x_ref, go_ref)
    feed(x_ref, go_ref, gate_ref, up_ref, down_ref, hid_ref, gl_ref, ul_ref)
    tg_ref[...] = ng_ref[...].astype(F32) + dot(x_ref[...], gl_ref[...], TN)
    tu_ref[...] = nu_ref[...].astype(F32) + dot(x_ref[...], ul_ref[...], TN)
    td_ref[...] = nd_ref[...].astype(F32) + dot(hid_ref[...], go_ref[...], TN)
    features, wide = tg_ref.shape
    tall, low = features // PARTS, wide // PARTS
    for n, bits in enumerate(orders):

        @pl.when(now == n)
        def _(n=n, bits=bits):
            for q, far in enumerate(away(bits or (0, 1, 2))):
                part = place_ref[0] ^ far if bits else far
                half = PARTS // 2
                out = packs[2 * n + q // half].at[q % half]
                rows = pl.ds(part * tall, tall)
                at = 0
                for grad_ref in (tg_ref, tu_ref):
                    for c in range(0, wide, LANES):
                        out[at : at + tall] = grad_ref[rows, c : c + LANES].astype(BF16)
                        at += tall
                rows = pl.ds(part * low, low)
                for c in range(0, features, LANES):
                    out[at : at + low] = td_ref[rows, c : c + LANES].astype(BF16)
                    at += low


def far_feed(place, xs, gos, gate, up, down, near_grads, before, orders, wide, index):
    rows, features = xs[0].shape
    tokens = 2 * rows
    hidden = gate.shape[1]
    blocks = len(orders)
    whole = pl.BlockSpec((rows, features), lambda i, _: (0, 0), pipeline_mode=pl.Buffered(1))
    col = pl.BlockSpec((features, wide), lambda i, _: (0, index + i))
    row = pl.BlockSpec((wide, features), lambda i, _: (index + i, 0))
    act = pl.BlockSpec((tokens, wide), lambda i, _: (0, index + i))
    packed = 3 * features * wide // PARTS // LANES
    half = pl.BlockSpec((PARTS // 2, packed, LANES), lambda i, _: (0, 0, 0), pipeline_mode=pl.Buffered(1))
    first = 1 + 4 + 3 + 3
    results = pl.pallas_call(
        functools.partial(far_kernel, orders),
        grid_spec=pltpu.PrefetchScalarGridSpec(
            num_scalar_prefetch=1,
            grid=(blocks,),
            in_specs=[whole] * 4
            + [col, col, row] * 2
            + [pl.BlockSpec(memory_space=pl.ANY)] * len(before),
            out_specs=[act] * 3 + [half] * (2 * blocks),
            scratch_shapes=[pltpu.VMEM((tokens, features), BF16)] * 2
            + [pltpu.VMEM((features, wide), F32)] * 2
            + [pltpu.VMEM((wide, features), F32)],
        ),
        out_shape=[jax.ShapeDtypeStruct((tokens, hidden), BF16)] * 3
        + [jax.ShapeDtypeStruct((PARTS // 2, packed, LANES), BF16)] * (2 * blocks),
        input_output_aliases={first + n: n for n in range(len(before))},
        compiler_params=pltpu.CompilerParams(vmem_limit_bytes=VMEM_LIMIT),
        cost_estimate=pl.CostEstimate(
            flops=12 * blocks * tokens * features * wide,
            transcendentals=0,
            bytes_accessed=18 * blocks * features * wide,
        ),
        name="far_feed",
    )(place, *xs, *gos, gate, up, down, *near_grads, *before)
    acts = results[:3]
    return acts, list(zip(results[3::2], results[4::2]))


def unpack_kernel(bits, pieces, place_ref, *refs):
    og_ref, ou_ref, od_ref = refs[-3:]
    features, wide = og_ref.shape
    tall, low = features // PARTS, wide // PARTS
    sources = [ref.at[n] for ref in refs[:pieces] for n in range(ref.shape[0])]
    for source, far in zip(sources, away(bits or (0, 1, 2))):
        part = place_ref[0] ^ far if bits else far
        rows = pl.ds(part * tall, tall)
        at = 0
        for out in (og_ref, ou_ref):
            for c in range(0, wide, LANES):
                out[rows, c : c + LANES] = source[at : at + tall].astype(F32)
                at += tall
        rows = pl.ds(part * low, low)
        for c in range(0, features, LANES):
            od_ref[rows, c : c + LANES] = source[at : at + low].astype(F32)
            at += low


def unpack(place, pieces, before, bits, wide, index, features, hidden):
    packed = pieces[0].shape[1]
    ins = [
        pl.BlockSpec((piece.shape[0], packed, LANES), lambda i, _: (0, 0, 0)) for piece in pieces
    ]
    col = pl.BlockSpec((features, wide), lambda i, _: (0, index))
    row = pl.BlockSpec((wide, features), lambda i, _: (index, 0))
    keep = [pl.BlockSpec(memory_space=pl.ANY)] * len(before)
    return pl.pallas_call(
        functools.partial(unpack_kernel, bits, len(pieces)),
        grid_spec=pltpu.PrefetchScalarGridSpec(
            num_scalar_prefetch=1,
            grid=(1,),
            in_specs=ins + keep,
            out_specs=[col, col, row],
        ),
        out_shape=[jax.ShapeDtypeStruct((features, hidden), F32)] * 2
        + [jax.ShapeDtypeStruct((hidden, features), F32)],
        input_output_aliases={1 + len(ins) + n: n for n in range(len(before))},
        compiler_params=pltpu.CompilerParams(vmem_limit_bytes=VMEM_LIMIT),
        cost_estimate=pl.CostEstimate(
            flops=0, transcendentals=0, bytes_accessed=1000
        ),
        name="unpack",
    )(place, *pieces, *before)


def add_low(one, two):
    return (one.astype(F32) + two.astype(F32)).astype(BF16)


def gather_mp(own):
    size = lax.axis_size("mp")
    blocks = [own] + [None] * (size - 1)
    for bit in reversed(range(bits_of("mp"))):
        for r in [r for r in range(size) if blocks[r] is not None]:
            blocks[r ^ (1 << bit)] = swap(blocks[r], "mp", bit)
    return blocks


class Sum:
    def __init__(self, kept, sent, bits):
        self.kept, self.sent, self.bits, self.step = kept, sent, bits, 0

    def send(self, *before):
        if before:
            self.sent = after(self.sent, *before)
        steps = len(self.bits)
        bit = self.bits[self.step] if self.step < steps else self.bits[2 * steps - 1 - self.step]
        self.got = swap(self.sent, "dp", bit)

    def add(self):
        self.step += 1
        got, steps = self.got, len(self.bits)
        if self.step < steps:
            half = self.kept.shape[0] // 2
            self.sent = add_low(self.kept[half:], got[half:])
            self.kept = add_low(self.kept[:half], got[:half])
        elif self.step == steps:
            own = add_low(self.kept, got)
            for bit in range(HALVINGS, bits_of("dp")):
                own = add_low(own, swap(own, "dp", bit))
            self.pieces = [own]
            self.sent = own
        else:
            self.pieces.append(got)
            if self.step < 2 * steps:
                self.sent = jnp.concatenate(self.pieces, 0)
        return self.sent


def scatter_all(array):
    steps = [("mp", b) for b in range(bits_of("mp"))] + [("dp", b) for b in range(bits_of("dp"))]
    count = len(steps)
    rows = array.shape[0] >> count
    array = array.reshape(array.shape[0] // rows, rows, array.shape[1])
    for axis, bit in steps:
        pairs = array.reshape(array.shape[0] // 2, 2, rows, array.shape[2])
        mine = bit_of(axis, bit)
        sent = lax.dynamic_index_in_dim(pairs, 1 - mine, 1, keepdims=False)
        kept = lax.dynamic_index_in_dim(pairs, mine, 1, keepdims=False)
        array = add_low(kept, swap(sent, axis, bit))
    return array[0]


def per_device(
    block_in,
    segment_ids,
    first_gain,
    in_proj,
    conv_kernel,
    out_proj,
    second_gain,
    gate_proj,
    up_proj,
    down_proj,
    out_grad,
):
    rows = block_in.shape[1]
    features = block_in.shape[2]
    lookback = KERNEL - 1
    x = block_in.reshape(rows, features).astype(F32)
    own_ids = segment_ids.reshape(rows)
    cotangent = out_grad.reshape(rows, features)

    small = jnp.concatenate(
        [first_gain[:, None], second_gain[:, None], conv_kernel], 1
    )
    small = jnp.pad(small, ((0, 0), (0, LANES - small.shape[1])))
    packed = jnp.concatenate([in_proj, out_proj, small], 1)
    everything = lax.all_gather(packed, ("dp", "mp"), axis=0, tiled=True)
    weight_in = everything[:, : 3 * features]
    weight_out = everything[:, 3 * features : 4 * features]
    vectors = everything[:, 4 * features : 4 * features + 2 + KERNEL].astype(F32).T
    gain_one, gain_two, taps = vectors[0], vectors[1], vectors[2:]

    group_grad = gather_mp(cotangent)
    everything = after(everything, group_grad)

    pad = 8
    rim = shift(block_in.reshape(rows, features)[rows - pad :], "mp", 1)
    rim_ids = shift(own_ids[rows - pad :].astype(F32), "mp", 1).astype(jnp.int32)
    rim_ids = jnp.where(lax.axis_index("mp") == 0, -1, rim_ids)
    x_all = jnp.concatenate([rim.astype(F32), x], 0)
    inverse_all = lax.rsqrt(jnp.mean(x_all * x_all, axis=-1, keepdims=True) + epsilon)
    low_all = (x_all * inverse_all * gain_one).astype(BF16)
    mixer_all = jnp.dot(low_all, weight_in, preferred_element_type=F32)
    extended = mixer_all[:, :features] * mixer_all[:, 2 * features :]
    inverse_one = inverse_all[pad:]
    unit_one = x * inverse_one
    first_low = low_all[pad:]
    mixer = mixer_all[pad:]
    opening = mixer[:, :features]
    closing = mixer[:, features : 2 * features]
    carried = mixer[:, 2 * features :]
    extended_ids = jnp.concatenate([rim_ids, own_ids], 0)
    skip = pad - lookback
    same = [
        (extended_ids[skip + k : skip + k + rows] == own_ids)[:, None] for k in range(KERNEL)
    ]
    past = [
        jnp.where(same[k], extended[skip + k : skip + k + rows], 0.0) for k in range(KERNEL)
    ]
    conv = sum(past[k] * taps[k] for k in range(KERNEL))
    gated_low = (closing * conv).astype(BF16)
    residual = x + jnp.dot(gated_low, weight_out, preferred_element_type=F32)
    inverse_two = lax.rsqrt(jnp.mean(residual * residual, axis=-1, keepdims=True) + epsilon)
    second_low = (residual * inverse_two * gain_two).astype(BF16)

    hidden_units = gate_proj.shape[1]
    place = (lax.axis_index("dp") % PARTS).reshape(1).astype(jnp.int32)
    beside = swap(second_low, "mp", 0)
    across = swap(second_low, "mp", 1)
    hid_near, gl_near, ul_near, *near_grads = near_feed(
        [second_low, beside], group_grad[:2], gate_proj, up_proj, down_proj
    )
    across = after(across, near_grads[0])
    far = (
        place, [across, swap(across, "mp", 0)], group_grad[2:], gate_proj, up_proj, down_proj,
        near_grads,
    )
    wide = hidden_units // 3
    assert wide % LANES == 0
    acts, sums = (), []
    for n in range(3):
        acts, [pair] = far_feed(*far, acts, [(0, 1, 2)], wide, n)
        sums.append(Sum(*pair, (0, 1, 2)))
        if n == 0:
            sums[0].send()
    hid_far, gl_far, ul_far = acts

    def back(gate_low, up_low):
        return (inner_cols(gate_low, gate_proj) + inner_cols(up_low, up_proj)).astype(BF16)

    def onward(hid):
        return dot(hid, down_proj, NN).astype(BF16)

    back_far = back(gl_far, ul_far)
    ready = sums[0].add()
    back_far = after(back_far, ready)
    sums[0].send()
    sums[1].send(ready)
    back_far = add_low(back_far[:rows], swap(back_far[rows:], "mp", 0))
    back_across = swap(back_far, "mp", 1)
    gl_near, ul_near = after((gl_near, ul_near), back_far)
    back_near = back(gl_near, ul_near)
    back_beside = swap(back_near[rows:], "mp", 0)
    ready = sums[0].add()
    sums[0].send()
    hid_near, hid_far = after((hid_near, hid_far), ready, back_near)
    on_near, on_far = onward(hid_near), onward(hid_far)
    on_beside = swap(on_near[rows:], "mp", 0)
    on_far = add_low(on_far[:rows], swap(on_far[rows:], "mp", 0))
    ready = sums[0].add(), sums[1].add(), on_far, on_beside
    sums[0].send()
    sums[1].send()
    sums[2].send(*ready)
    back_across = after(back_across, *ready)
    second_grad = back_near[:rows].astype(F32) + back_beside.astype(F32) + back_across.astype(F32)
    on_across = swap(after(on_far, back_across), "mp", 1)
    branch = on_near[:rows].astype(F32) + on_beside.astype(F32) + on_across.astype(F32)
    layer_out = (residual + branch).astype(BF16).reshape(1, rows, features)

    unit_two = residual * inverse_two
    weighted = second_grad * gain_two
    residual_grad = cotangent.astype(F32) + inverse_two * (
        weighted - unit_two * jnp.mean(weighted * unit_two, axis=-1, keepdims=True)
    )
    second_local = jnp.sum(second_grad * unit_two, axis=0)
    residual_low = residual_grad.astype(BF16)
    ready = sums[0].add(), sums[1].add()
    sums[0].send()
    sums[1].send()
    residual_low = after(residual_low, *ready)
    out_local = inner_rows(gated_low, residual_low)
    gated_grad = inner_cols(residual_low, weight_out)
    closing_grad = gated_grad * conv
    conv_grad = gated_grad * closing
    kernel_local = [jnp.sum(conv_grad * past[k], axis=0) for k in range(KERNEL)]
    spread = jnp.zeros((rows + lookback, features), F32)
    spread = sum(
        jnp.pad(jnp.where(same[k], conv_grad * taps[k], 0.0), ((k, lookback - k), (0, 0)))
        for k in range(KERNEL)
    )
    rim_back = shift(spread[:lookback], "mp", -1)
    product_grad = spread[lookback:] + jnp.pad(rim_back, ((rows - lookback, 0), (0, 0)))
    mixer_grad = jnp.concatenate(
        [product_grad * carried, closing_grad, product_grad * opening], 1
    ).astype(BF16)
    ready = sums[0].add(), sums[1].add(), sums[2].add()
    sums[0].send(ready[2])
    sums[1].send()
    sums[2].send()
    mixer_grad = after(mixer_grad, *ready)
    in_local = inner_rows(first_low, mixer_grad).astype(BF16)
    first_grad = inner_cols(mixer_grad, weight_in)
    weighted = first_grad * gain_one
    input_grad = residual_grad + inverse_one * (
        weighted - unit_one * jnp.mean(weighted * unit_one, axis=-1, keepdims=True)
    )
    input_grad = input_grad.reshape(1, rows, features)

    for _ in range(5):
        for one in sums:
            if one.step < 5:
                one.add()
                one.send()
    done = ()
    for n, one in enumerate(sums):
        one.add()
        done = unpack(place, one.pieces, done, (0, 1, 2), wide, n, features, hidden_units)
    grad_gate, grad_up, grad_down = done

    small_local = jnp.stack([second_local] + kernel_local, 1).astype(BF16)
    small_local = jnp.pad(small_local, ((0, 0), (0, LANES - small_local.shape[1])))
    early = scatter_all(jnp.concatenate([out_local.astype(BF16), small_local], 1)).astype(F32)
    grad_out = early[:, :features]
    grad_second = early[:, features]
    grad_conv = early[:, features + 1 : features + 1 + KERNEL]
    grad_in = scatter_all(in_local).astype(F32)
    grad_first = jnp.sum(grad_in * in_proj.astype(F32), axis=1) / first_gain.astype(F32)
    return (
        layer_out,
        input_grad,
        grad_first,
        grad_in,
        grad_conv,
        grad_out,
        grad_second,
        grad_gate,
        grad_up,
        grad_down,
    )


def solution(mesh):
    in_specs = (
        P("dp", "mp", None),
        P("dp", "mp"),
        P(("dp", "mp")),
        P(("dp", "mp"), None),
        P(("dp", "mp"), None),
        P(("dp", "mp"), None),
        P(("dp", "mp")),
        P(None, "mp"),
        P(None, "mp"),
        P("mp", None),
        P("dp", "mp", None),
    )
    out_specs = (
        P("dp", "mp", None),
        P("dp", "mp", None),
        P(("dp", "mp")),
        P(("dp", "mp"), None),
        P(("dp", "mp"), None),
        P(("dp", "mp"), None),
        P(("dp", "mp")),
        P(None, "mp"),
        P(None, "mp"),
        P("mp", None),
    )
    return jax.shard_map(
        per_device, mesh=mesh, in_specs=in_specs, out_specs=out_specs, check_vma=False
    )
```

```python
import functools

import jax
import jax.numpy as jnp
from jax import lax
from jax.experimental import pallas as pl
from jax.experimental.pallas import tpu as pltpu
from jax.sharding import PartitionSpec as P

KERNEL = 3
LANES = 128
BF16 = jnp.bfloat16
F32 = jnp.float32
HALVINGS = 3
PARTS = 1 << HALVINGS
NN = (((1,), (0,)), ((), ()))
NT = (((1,), (1,)), ((), ()))
TN = (((0,), (0,)), ((), ()))
VMEM_LIMIT = 60 * 1024 * 1024
LONG = pl.CostEstimate(flops=10**11, transcendentals=0, bytes_accessed=0)

epsilon = 1e-05


def swap(block, axis, bit):
    size = lax.axis_size(axis)
    return lax.ppermute(block, axis, [(i, i ^ (1 << bit)) for i in range(size)])


def shift(block, axis, distance):
    devices = range(lax.axis_size(axis))
    route = [(i - distance, i) for i in devices if i - distance in devices]
    return lax.ppermute(block, axis, route)


def bit_of(axis, bit):
    return (lax.axis_index(axis) >> bit) & 1


def bits_of(axis):
    size = lax.axis_size(axis)
    assert size & (size - 1) == 0
    return size.bit_length() - 1


def after(values, *before):
    return lax.optimization_barrier((values, before))[0]


class Order:
    def __init__(self):
        self.last = ()

    def __call__(self, values):
        return after(values, self.last)

    def mark(self, out):
        self.last = out
        return out


def away(bits):
    top = len(bits) - 1
    return [sum(((q >> (top - n)) & 1) << bit for n, bit in enumerate(bits)) for q in range(PARTS)]


def dot(left, right, dims):
    return lax.dot_general(left, right, dims, preferred_element_type=F32)


def activate(gate_val, up_val, hidden_grad):
    sig = 1.0 / (1.0 + jnp.exp(-gate_val))
    silu = gate_val * sig
    return (
        (silu * up_val).astype(BF16),
        (hidden_grad * up_val * (sig * (1.0 + gate_val * (1.0 - sig)))).astype(BF16),
        (hidden_grad * silu).astype(BF16),
    )


def feed(x_ref, go_ref, gate_ref, up_ref, down_ref, acts, outs):
    for n in range(2):
        step = x_ref.shape[0] // 2
        part = slice(n * step, (n + 1) * step)
        gate_val = dot(x_ref[part], gate_ref[...], NN)
        up_val = dot(x_ref[part], up_ref[...], NN)
        hidden_grad = dot(go_ref[part], down_ref[...], NT)
        for m, value in enumerate(activate(gate_val, up_val, hidden_grad)):
            acts[m][part] = value
            outs[2 * m + n][...] = value


def join(first, xa_ref, xb_ref, ga_ref, gb_ref, x_ref, go_ref):
    rows = xa_ref.shape[0]

    @pl.when(first)
    def _():
        x_ref[:rows] = xa_ref[...]
        x_ref[rows:] = xb_ref[...]
        go_ref[:rows] = ga_ref[...]
        go_ref[rows:] = gb_ref[...]


def near_kernel(xa_ref, xb_ref, ga_ref, gb_ref, gate_ref, up_ref, down_ref,
                *refs):
    outs = refs[:6]
    og_ref, ou_ref, od_ref, x_ref, go_ref, hid_ref, gl_ref, ul_ref = refs[6:]
    join(pl.program_id(0) == 0, xa_ref, xb_ref, ga_ref, gb_ref, x_ref, go_ref)
    feed(x_ref, go_ref, gate_ref, up_ref, down_ref, (hid_ref, gl_ref, ul_ref), outs)
    og_ref[...] = dot(x_ref[...], gl_ref[...], TN).astype(BF16)
    ou_ref[...] = dot(x_ref[...], ul_ref[...], TN).astype(BF16)
    od_ref[...] = dot(hid_ref[...], go_ref[...], TN).astype(BF16)


def near_feed(xs, gos, gate, up, down):
    rows, features = xs[0].shape
    hidden = gate.shape[1]
    wide = 256
    tokens = 2 * rows
    whole = pl.BlockSpec((rows, features), lambda i: (0, 0), pipeline_mode=pl.Buffered(1))
    col = pl.BlockSpec((features, wide), lambda i: (0, i))
    row = pl.BlockSpec((wide, features), lambda i: (i, 0))
    act = pl.BlockSpec((rows, wide), lambda i: (0, i))
    return pl.pallas_call(
        near_kernel,
        grid=(pl.cdiv(hidden, wide),),
        in_specs=[whole] * 4 + [col, col, row],
        out_specs=[act] * 6 + [col, col, row],
        out_shape=[jax.ShapeDtypeStruct((rows, hidden), BF16)] * 6
        + [jax.ShapeDtypeStruct((features, hidden), BF16)] * 2
        + [jax.ShapeDtypeStruct((hidden, features), BF16)],
        scratch_shapes=[pltpu.VMEM((tokens, features), BF16)] * 2
        + [pltpu.VMEM((tokens, wide), BF16)] * 3,
        compiler_params=pltpu.CompilerParams(vmem_limit_bytes=VMEM_LIMIT),
        cost_estimate=LONG,
        name="near_feed",
    )(*xs, *gos, gate, up, down)


def far_kernel(orders, place_ref, xa_ref, xb_ref, ga_ref, gb_ref, gate_ref, up_ref, down_ref,
               ng_ref, nu_ref, nd_ref, *refs):
    blocks = len(orders)
    x_ref, go_ref, tg_ref, tu_ref, td_ref, hid_ref, gl_ref, ul_ref = refs[-8:]
    packs = refs[-8 - 2 * blocks : -8]
    outs = refs[-14 - 2 * blocks : -8 - 2 * blocks]
    now = pl.program_id(0)
    join(now == 0, xa_ref, xb_ref, ga_ref, gb_ref, x_ref, go_ref)
    feed(x_ref, go_ref, gate_ref, up_ref, down_ref, (hid_ref, gl_ref, ul_ref), outs)
    tg_ref[...] = ng_ref[...].astype(F32) + dot(x_ref[...], gl_ref[...], TN)
    tu_ref[...] = nu_ref[...].astype(F32) + dot(x_ref[...], ul_ref[...], TN)
    td_ref[...] = nd_ref[...].astype(F32) + dot(hid_ref[...], go_ref[...], TN)
    features, wide = tg_ref.shape
    tall, low = features // PARTS, wide // PARTS
    for n, bits in enumerate(orders):

        @pl.when(now == n)
        def _(n=n, bits=bits):
            for q, far in enumerate(away(bits or (0, 1, 2))):
                part = place_ref[0] ^ far if bits else far
                half = PARTS // 2
                out = packs[2 * n + q // half].at[q % half]
                rows = pl.ds(part * tall, tall)
                at = 0
                for grad_ref in (tg_ref, tu_ref):
                    for c in range(0, wide, LANES):
                        out[at : at + tall] = grad_ref[rows, c : c + LANES].astype(BF16)
                        at += tall
                rows = pl.ds(part * low, low)
                for c in range(0, features, LANES):
                    out[at : at + low] = td_ref[rows, c : c + LANES].astype(BF16)
                    at += low


def far_feed(place, xs, gos, gate, up, down, near_grads, before, orders, wide, index):
    rows, features = xs[0].shape
    tokens = 2 * rows
    hidden = gate.shape[1]
    blocks = len(orders)
    whole = pl.BlockSpec((rows, features), lambda i, _: (0, 0), pipeline_mode=pl.Buffered(1))
    col = pl.BlockSpec((features, wide), lambda i, _: (0, index + i))
    row = pl.BlockSpec((wide, features), lambda i, _: (index + i, 0))
    act = pl.BlockSpec((rows, wide), lambda i, _: (0, index + i))
    packed = 3 * features * wide // PARTS // LANES
    half = pl.BlockSpec((PARTS // 2, packed, LANES), lambda i, _: (0, 0, 0), pipeline_mode=pl.Buffered(1))
    first = 1 + 4 + 3 + 3
    results = pl.pallas_call(
        functools.partial(far_kernel, orders),
        grid_spec=pltpu.PrefetchScalarGridSpec(
            num_scalar_prefetch=1,
            grid=(blocks,),
            in_specs=[whole] * 4
            + [col, col, row] * 2
            + [pl.BlockSpec(memory_space=pl.ANY)] * len(before),
            out_specs=[act] * 6 + [half] * (2 * blocks),
            scratch_shapes=[pltpu.VMEM((tokens, features), BF16)] * 2
            + [pltpu.VMEM((features, wide), F32)] * 2
            + [pltpu.VMEM((wide, features), F32)]
            + [pltpu.VMEM((tokens, wide), BF16)] * 3,
        ),
        out_shape=[jax.ShapeDtypeStruct((rows, hidden), BF16)] * 6
        + [jax.ShapeDtypeStruct((PARTS // 2, packed, LANES), BF16)] * (2 * blocks),
        input_output_aliases={first + n: n for n in range(len(before))},
        compiler_params=pltpu.CompilerParams(vmem_limit_bytes=VMEM_LIMIT),
        cost_estimate=LONG,
        name="far_feed",
    )(place, *xs, *gos, gate, up, down, *near_grads, *before)
    return results[:6], list(zip(results[6::2], results[7::2]))


def unpack_kernel(bits, pieces, place_ref, *refs):
    og_ref, ou_ref, od_ref = refs[-3:]
    features, wide = og_ref.shape
    tall, low = features // PARTS, wide // PARTS
    sources = [ref.at[n] for ref in refs[:pieces] for n in range(ref.shape[0])]
    for source, far in zip(sources, away(bits or (0, 1, 2))):
        part = place_ref[0] ^ far if bits else far
        rows = pl.ds(part * tall, tall)
        at = 0
        for out in (og_ref, ou_ref):
            for c in range(0, wide, LANES):
                out[rows, c : c + LANES] = source[at : at + tall].astype(F32)
                at += tall
        rows = pl.ds(part * low, low)
        for c in range(0, features, LANES):
            od_ref[rows, c : c + LANES] = source[at : at + low].astype(F32)
            at += low


def unpack(place, pieces, before, bits, wide, index, features, hidden):
    packed = pieces[0].shape[1]
    ins = [
        pl.BlockSpec((piece.shape[0], packed, LANES), lambda i, _: (0, 0, 0)) for piece in pieces
    ]
    col = pl.BlockSpec((features, wide), lambda i, _: (0, index))
    row = pl.BlockSpec((wide, features), lambda i, _: (index, 0))
    keep = [pl.BlockSpec(memory_space=pl.ANY)] * len(before)
    return pl.pallas_call(
        functools.partial(unpack_kernel, bits, len(pieces)),
        grid_spec=pltpu.PrefetchScalarGridSpec(
            num_scalar_prefetch=1,
            grid=(1,),
            in_specs=ins + keep,
            out_specs=[col, col, row],
        ),
        out_shape=[jax.ShapeDtypeStruct((features, hidden), F32)] * 2
        + [jax.ShapeDtypeStruct((hidden, features), F32)],
        input_output_aliases={1 + len(ins) + n: n for n in range(len(before))},
        compiler_params=pltpu.CompilerParams(vmem_limit_bytes=VMEM_LIMIT),
        cost_estimate=LONG,
        name="unpack",
    )(place, *pieces, *before)


def add_low(one, two):
    return (one.astype(F32) + two.astype(F32)).astype(BF16)


def whole(array):
    return pl.BlockSpec(array.shape, lambda i: (0,) * array.ndim)


def halve_kernel(kept_ref, got_ref, *outs):
    half = outs[-1].shape[0]
    for n, out in enumerate(outs):
        part = slice(n * half, (n + 1) * half)
        out[...] = (kept_ref[part].astype(F32) + got_ref[part].astype(F32)).astype(out.dtype)


def halve(kept, got, halves=2, dtype=BF16):
    count, tall, wide = kept.shape
    shapes = [jax.ShapeDtypeStruct((count // halves, tall, wide), dtype)] * halves
    return pl.pallas_call(
        halve_kernel,
        grid=(1,),
        in_specs=[whole(kept), whole(got)],
        out_specs=[whole(s) for s in shapes],
        out_shape=shapes,
        compiler_params=pltpu.CompilerParams(vmem_limit_bytes=VMEM_LIMIT),
        cost_estimate=LONG,
        name="halve",
    )(kept, got)


def lay_kernel(*refs):
    at = 0
    for ref in refs[:-1]:
        refs[-1][at : at + ref.shape[0]] = ref[...]
        at += ref.shape[0]


def lay(pieces):
    _, tall, wide = pieces[0].shape
    shape = jax.ShapeDtypeStruct((sum(p.shape[0] for p in pieces), tall, wide), pieces[0].dtype)
    return pl.pallas_call(
        lay_kernel,
        grid=(1,),
        in_specs=[whole(p) for p in pieces],
        out_specs=whole(shape),
        out_shape=shape,
        compiler_params=pltpu.CompilerParams(vmem_limit_bytes=VMEM_LIMIT),
        cost_estimate=LONG,
        name="lay",
    )(*pieces)


def pack_rows(place, bits, grad_ref, kept_ref, sent_ref, lane):
    count = len(bits)
    half, tall, _ = kept_ref.shape
    wide = grad_ref.shape[1]

    def move(q, out_ref, slot):
        far = 0
        for n, bit in enumerate(bits):
            far = far | (((q >> (count - 1 - n)) & 1) << bit)
        rows = pl.ds(pl.multiple_of((place ^ far) * tall, tall), tall)
        out_ref[slot, :, lane : lane + wide] = grad_ref[rows].astype(BF16)

    @pl.loop(0, half)
    def _(q):
        move(q, kept_ref, q)
        move(q + half, sent_ref, q)


STRIP = 64
RIM = 8


def fold(values):
    return jnp.sum(values.reshape(values.shape[0] // 8, 8, values.shape[1]), axis=0)


def assemble(place, bits, sources, width, target_ref, lane, sems):
    half, tall, _ = sources[0][0].shape
    count = len(bits)

    def copy(q, n):
        ref, start = sources[n]
        far = 0
        for m, bit in enumerate(bits):
            far = far | ((((q + n * half) >> m) & 1) << bit)
        rows = pl.ds(pl.multiple_of((place ^ far) * tall, tall), tall)
        return pltpu.make_async_copy(
            ref.at[q, :, start : start + width],
            target_ref.at[rows, lane : lane + width],
            sems.at[n * half + q],
        )

    @pl.loop(0, half)
    def _(q):
        for n in range(2):
            copy(q, n).start()

    def wait():
        @pl.loop(0, half)
        def _(q):
            for n in range(2):
                copy(q, n).wait()

    return wait


def mix_front_kernel(bits, place_ref, in_any, c0, c1, x_ref, before_ref, same_ref,
                     mix_any, low_any, gated_any, vec_ref, res_ref, second_ref,
                     w_ref, wo_ref, mix_ref, low_ref, gated_ref, ext_ref, sems, in_sem, out_sem):
    place = place_ref[0]
    rows, features = x_ref.shape
    last = features + LANES
    wide = features
    loads = [
        pltpu.make_async_copy(
            in_any.at[:, n * wide : (n + 1) * wide], w_ref.at[:, n * wide : (n + 1) * wide], in_sem.at[n]
        )
        for n in range(3)
    ]
    wait_out = assemble(place, bits, [(c0, 0), (c1, 0)], features + LANES, wo_ref, 0, sems)
    for load in loads:
        load.start()
    wait_out()
    vec_ref[...] = wo_ref[:, features:].astype(F32).T[:8]
    gain_one, gain_two = vec_ref[0:1], vec_ref[1:2]
    taps = [vec_ref[2 + k : 3 + k] for k in range(KERNEL)]

    def normed(values, gain):
        inverse = lax.rsqrt(jnp.mean(values * values, axis=-1, keepdims=True) + epsilon)
        return (values * inverse * gain).astype(BF16)

    low_ref[:RIM] = normed(before_ref[...].astype(F32), gain_one)

    @pl.loop(0, rows // STRIP)
    def _(i):
        at = pl.ds(pl.multiple_of(i * STRIP, STRIP), STRIP)
        inner = pl.ds(pl.multiple_of(i * STRIP + RIM, RIM), STRIP)
        low_ref[inner] = normed(x_ref[at].astype(F32), gain_one)

    stores = [pltpu.make_async_copy(low_ref, low_any, out_sem.at[0])]
    stores[0].start()
    for n, load in enumerate(loads):
        load.wait()
        part = slice(n * wide, (n + 1) * wide)
        mix_ref[:, part] = dot(low_ref[...], w_ref[:, part], NN)
        stores.append(
            pltpu.make_async_copy(mix_ref.at[:, part], mix_any.at[:, part], out_sem.at[1 + n])
        )
        stores[-1].start()
    ext_ref[:RIM] = mix_ref[:RIM, :features] * mix_ref[:RIM, 2 * features :]

    @pl.loop(0, rows // STRIP)
    def _(i):
        at = pl.ds(pl.multiple_of(i * STRIP + RIM, RIM), STRIP)
        ext_ref[at] = mix_ref[at, :features] * mix_ref[at, 2 * features :]

    @pl.loop(0, rows // STRIP)
    def _(i):
        at = pl.ds(pl.multiple_of(i * STRIP, STRIP), STRIP)
        inner = pl.ds(pl.multiple_of(i * STRIP + RIM, RIM), STRIP)
        window = ext_ref[pl.ds(pl.multiple_of(i * STRIP, STRIP), STRIP + RIM)]
        skip = RIM - (KERNEL - 1)
        conv = 0.0
        for k in range(KERNEL):
            same = same_ref[at, k : k + 1] > 0.5
            conv += jnp.where(same, window[skip + k : skip + k + STRIP], 0.0) * taps[k]
        gated_ref[at] = (mix_ref[inner, features : 2 * features] * conv).astype(BF16)

    stores.append(pltpu.make_async_copy(gated_ref, gated_any, out_sem.at[4]))
    stores[-1].start()
    res_ref[...] = dot(gated_ref[...], wo_ref[:, :features], NN)

    @pl.loop(0, rows // STRIP)
    def _(i):
        at = pl.ds(pl.multiple_of(i * STRIP, STRIP), STRIP)
        residual = x_ref[at].astype(F32) + res_ref[at]
        res_ref[at] = residual
        second_ref[at] = normed(residual, gain_two)

    for store in stores:
        store.wait()


def mix_front(place, bits, weight_in, gathered, x, before, same):
    rows, features = x.shape
    anywhere = pl.BlockSpec(memory_space=pl.ANY)
    outs = [
        jax.ShapeDtypeStruct((rows + RIM, 3 * features), F32),
        jax.ShapeDtypeStruct((rows + RIM, features), BF16),
        jax.ShapeDtypeStruct((rows, features), BF16),
        jax.ShapeDtypeStruct((8, features), F32),
        jax.ShapeDtypeStruct((rows, features), F32),
        jax.ShapeDtypeStruct((rows, features), BF16),
    ]
    return pl.pallas_call(
        functools.partial(mix_front_kernel, bits),
        grid_spec=pltpu.PrefetchScalarGridSpec(
            num_scalar_prefetch=1,
            grid=(1,),
            in_specs=[anywhere] * 3 + [once(x), once(before), once(same)],
            out_specs=[anywhere] * 3 + [once(s) for s in outs[3:]],
            scratch_shapes=[
                pltpu.VMEM((features, 3 * features), BF16),
                pltpu.VMEM((features, features + LANES), BF16),
                pltpu.VMEM((rows + RIM, 3 * features), F32),
                pltpu.VMEM((rows + RIM, features), BF16),
                pltpu.VMEM((rows, features), BF16),
                pltpu.VMEM((rows + RIM, features), F32),
                pltpu.SemaphoreType.DMA((1 << len(bits),)),
                pltpu.SemaphoreType.DMA((3,)),
                pltpu.SemaphoreType.DMA((5,)),
            ],
        ),
        out_shape=outs,
        compiler_params=pltpu.CompilerParams(vmem_limit_bytes=VMEM_LIMIT),
        cost_estimate=LONG,
        name="mix_front",
    )(place, weight_in, *gathered, x, before, same)


def mix_back_kernel(bits, place_ref, near_ref, beside_ref, across_ref, cot_ref, res_ref, mix_ref,
                    c0, c1, vec_ref, same_ref,
                    rg_ref, rlow_ref, cl_ref, pg_ref, rim_ref, sums_ref,
                    ext_ref, gg_ref, d0_ref, d1_ref, d2_ref, w_ref, sems):
    rows, features = res_ref.shape
    wait = assemble(place_ref[0], bits, [(c0, 0), (c1, 0)], features, w_ref, 0, sems)
    sums_ref[...] = jnp.zeros_like(sums_ref)
    gain = vec_ref[1:2]
    taps = [vec_ref[2 + k : 3 + k] for k in range(KERNEL)]

    @pl.loop(0, rows // STRIP)
    def _(i):
        at = pl.ds(pl.multiple_of(i * STRIP, STRIP), STRIP)
        second = near_ref[at].astype(F32) + beside_ref[at].astype(F32) + across_ref[at].astype(F32)
        residual = res_ref[at]
        inverse = lax.rsqrt(jnp.mean(residual * residual, axis=-1, keepdims=True) + epsilon)
        unit = residual * inverse
        weighted = second * gain
        mean = jnp.mean(weighted * unit, axis=-1, keepdims=True)
        grad = cot_ref[at].astype(F32) + inverse * (weighted - unit * mean)
        rg_ref[at] = grad
        rlow_ref[at] = grad.astype(BF16)
        sums_ref[0] += fold(second * unit)

    wait()
    gg_ref[...] = dot(rlow_ref[...], w_ref[...], NT)
    ext_ref[:RIM] = mix_ref[:RIM, :features] * mix_ref[:RIM, 2 * features :]

    @pl.loop(0, rows // STRIP)
    def _(i):
        at = pl.ds(pl.multiple_of(i * STRIP + RIM, RIM), STRIP)
        ext_ref[at] = mix_ref[at, :features] * mix_ref[at, 2 * features :]

    zeros = jnp.zeros((RIM, features), F32)
    for d_ref in (d0_ref, d1_ref, d2_ref):
        d_ref[:RIM] = zeros
        d_ref[rows + RIM :] = zeros

    @pl.loop(0, rows // STRIP)
    def _(i):
        at = pl.ds(pl.multiple_of(i * STRIP, STRIP), STRIP)
        inner = pl.ds(pl.multiple_of(i * STRIP + RIM, RIM), STRIP)
        window = ext_ref[pl.ds(pl.multiple_of(i * STRIP, STRIP), STRIP + RIM)]
        skip = RIM - (KERNEL - 1)
        same = [same_ref[at, k : k + 1] > 0.5 for k in range(KERNEL)]
        past = [
            jnp.where(same[k], window[skip + k : skip + k + STRIP], 0.0) for k in range(KERNEL)
        ]
        conv = past[0] * taps[0] + past[1] * taps[1] + past[2] * taps[2]
        gated_grad = gg_ref[at]
        cl_ref[at] = (gated_grad * conv).astype(BF16)
        conv_grad = gated_grad * mix_ref[inner, features : 2 * features]
        for k, d_ref in enumerate((d0_ref, d1_ref, d2_ref)):
            sums_ref[1 + k] += fold(conv_grad * past[k])
            d_ref[inner] = jnp.where(same[k], conv_grad * taps[k], 0.0)

    rim_ref[...] = d0_ref[2 : 2 + RIM] + d1_ref[1 : 1 + RIM]

    @pl.loop(0, rows // STRIP)
    def _(i):
        at = pl.ds(pl.multiple_of(i * STRIP, STRIP), STRIP)
        window = pl.ds(pl.multiple_of(i * STRIP + RIM, RIM), STRIP + RIM)
        inner = pl.ds(pl.multiple_of(i * STRIP + RIM, RIM), STRIP)
        pg_ref[at] = (
            d2_ref[inner] + d1_ref[window][1 : 1 + STRIP] + d0_ref[window][2 : 2 + STRIP]
        )


def mix_outer_kernel(bits, place_ref, gated_ref, rlow_ref, low_ref, cl_ref, sums_ref,
                     out_kept, out_sent, acc_ref):
    place = place_ref[0]
    features = acc_ref.shape[0]
    acc_ref[...] = dot(gated_ref[...], rlow_ref[...], TN)
    pack_rows(place, bits, acc_ref, out_kept, out_sent, 0)
    totals = jnp.sum(sums_ref[...], axis=1)
    totals = jnp.concatenate([totals, jnp.zeros_like(totals)], 0)[:8].astype(BF16)
    units = lax.broadcasted_iota(jnp.int32, (8, LANES), 0) == lax.broadcasted_iota(
        jnp.int32, (8, LANES), 1
    )
    acc_ref[:, :LANES] = dot(totals, jnp.where(units, 1.0, 0.0).astype(BF16), TN)
    pack_rows(place, bits, acc_ref.at[:, :LANES], out_kept, out_sent, features)
    acc_ref[...] = dot(low_ref[RIM:], cl_ref[...], TN)
    pack_rows(place, bits, acc_ref, out_kept, out_sent, features + LANES)


def once(array):
    return pl.BlockSpec(array.shape, lambda *_: (0,) * array.ndim, pipeline_mode=pl.Buffered(1))


def mix_back(place, bits, near, beside, across, cot, res, mix, gathered, vec, same):
    rows, features = res.shape
    shapes = [
        jax.ShapeDtypeStruct((rows, features), F32),
        jax.ShapeDtypeStruct((rows, features), BF16),
        jax.ShapeDtypeStruct((rows, features), BF16),
        jax.ShapeDtypeStruct((rows, features), F32),
        jax.ShapeDtypeStruct((RIM, features), F32),
        jax.ShapeDtypeStruct((1 + KERNEL, 8, features), F32),
    ]
    ins = [near, beside, across, cot, res, mix]
    anywhere = pl.BlockSpec(memory_space=pl.ANY)
    return pl.pallas_call(
        functools.partial(mix_back_kernel, bits),
        grid_spec=pltpu.PrefetchScalarGridSpec(
            num_scalar_prefetch=1,
            grid=(1,),
            in_specs=[once(a) for a in ins] + [anywhere] * 2 + [once(vec), once(same)],
            out_specs=[once(s) for s in shapes],
            scratch_shapes=[
                pltpu.VMEM((rows + RIM, features), F32),
                pltpu.VMEM((rows, features), F32),
                *[pltpu.VMEM((rows + 2 * RIM, features), F32)] * 3,
                pltpu.VMEM((features, features), BF16),
                pltpu.SemaphoreType.DMA((1 << len(bits),)),
            ],
        ),
        out_shape=shapes,
        compiler_params=pltpu.CompilerParams(vmem_limit_bytes=VMEM_LIMIT),
        cost_estimate=LONG,
        name="mix_back",
    )(place, *ins, *gathered, vec, same)


def mix_outer(place, bits, gated, rlow, low, cl, sums):
    features = gated.shape[1]
    parts = 1 << len(bits)
    ins = [gated, rlow, low, cl, sums]
    shapes = [
        jax.ShapeDtypeStruct((parts // 2, features // parts, 2 * features + LANES), BF16)
    ] * 2
    return pl.pallas_call(
        functools.partial(mix_outer_kernel, bits),
        grid_spec=pltpu.PrefetchScalarGridSpec(
            num_scalar_prefetch=1,
            grid=(1,),
            in_specs=[once(a) for a in ins],
            out_specs=[once(s) for s in shapes],
            scratch_shapes=[pltpu.VMEM((features, features), F32)],
        ),
        out_shape=shapes,
        compiler_params=pltpu.CompilerParams(vmem_limit_bytes=VMEM_LIMIT),
        cost_estimate=LONG,
        name="mix_outer",
    )(place, *ins)


def mix_grads_kernel(bits, place_ref, pg_ref, rim_ref, mix_ref, low_ref,
                     first_ref, last_ref, kept_ref, sent_ref, acc_ref):
    place = place_ref[0]
    rows, features = pg_ref.shape

    @pl.loop(0, rows // STRIP)
    def _(i):
        at = pl.ds(pl.multiple_of(i * STRIP, STRIP), STRIP)
        inner = pl.ds(pl.multiple_of(i * STRIP + RIM, RIM), STRIP)
        grad = pg_ref[at]
        first_ref[at] = (grad * mix_ref[inner, 2 * features :]).astype(BF16)
        last_ref[at] = (grad * mix_ref[inner, :features]).astype(BF16)

    grad = pg_ref[rows - RIM :] + rim_ref[...]
    first_ref[rows - RIM :] = (grad * mix_ref[rows:, 2 * features :]).astype(BF16)
    last_ref[rows - RIM :] = (grad * mix_ref[rows:, :features]).astype(BF16)
    for n, grad_ref in enumerate((first_ref, last_ref)):
        acc_ref[...] = dot(low_ref[RIM:], grad_ref[...], TN)
        pack_rows(place, bits, acc_ref, kept_ref, sent_ref, n * features)


def mix_grads(place, bits, pg, rim, mix, low):
    rows, features = pg.shape
    parts = 1 << len(bits)
    tall = features // parts

    def whole(array):
        return pl.BlockSpec(
            array.shape, lambda i, _: (0,) * array.ndim, pipeline_mode=pl.Buffered(1)
        )

    shapes = [jax.ShapeDtypeStruct((rows, features), BF16)] * 2
    shapes += [jax.ShapeDtypeStruct((parts // 2, tall, 2 * features), BF16)] * 2
    return pl.pallas_call(
        functools.partial(mix_grads_kernel, bits),
        grid_spec=pltpu.PrefetchScalarGridSpec(
            num_scalar_prefetch=1,
            grid=(1,),
            in_specs=[whole(a) for a in (pg, rim, mix, low)],
            out_specs=[whole(s) for s in shapes],
            scratch_shapes=[pltpu.VMEM((features, features), F32)],
        ),
        out_shape=shapes,
        compiler_params=pltpu.CompilerParams(vmem_limit_bytes=VMEM_LIMIT),
        cost_estimate=LONG,
        name="mix_grads",
    )(place, pg, rim, mix, low)


def input_back_kernel(first_ref, mid_ref, last_ref, w_ref, rg_ref, x_ref, vec_ref, out_ref, fg_ref):
    rows, features = rg_ref.shape
    fg_ref[...] = dot(first_ref[...], w_ref[:, :features], NT)
    fg_ref[...] += dot(mid_ref[...], w_ref[:, features : 2 * features], NT)
    fg_ref[...] += dot(last_ref[...], w_ref[:, 2 * features :], NT)

    @pl.loop(0, rows // STRIP)
    def _(i):
        at = pl.ds(pl.multiple_of(i * STRIP, STRIP), STRIP)
        values = x_ref[at].astype(F32)
        inverse = lax.rsqrt(jnp.mean(values * values, axis=-1, keepdims=True) + epsilon)
        unit = values * inverse
        weighted = fg_ref[at] * vec_ref[0:1]
        mean = jnp.mean(weighted * unit, axis=-1, keepdims=True)
        out_ref[at] = rg_ref[at] + inverse * (weighted - unit * mean)


def input_back(first, mid, last, weight_in, rg, x, vec):
    rows, features = rg.shape
    ins = [first, mid, last, weight_in, rg, x, vec]
    return pl.pallas_call(
        input_back_kernel,
        grid=(1,),
        in_specs=[once(a) for a in ins],
        out_specs=once(rg),
        out_shape=jax.ShapeDtypeStruct((rows, features), F32),
        scratch_shapes=[pltpu.VMEM((rows, features), F32)],
        compiler_params=pltpu.CompilerParams(vmem_limit_bytes=VMEM_LIMIT),
        cost_estimate=LONG,
        name="input_back",
    )(*ins)


def gather_mp(own):
    size = lax.axis_size("mp")
    blocks = [own] + [None] * (size - 1)
    for bit in reversed(range(bits_of("mp"))):
        for r in [r for r in range(size) if blocks[r] is not None]:
            blocks[r ^ (1 << bit)] = swap(blocks[r], "mp", bit)
    return blocks


class Sum:
    def __init__(self, order, kept, sent, bits):
        self.order, self.kept, self.sent, self.bits, self.step = order, kept, sent, bits, 0

    def send(self):
        steps = len(self.bits)
        bit = self.bits[self.step] if self.step < steps else self.bits[2 * steps - 1 - self.step]
        self.got = swap(self.sent, "dp", bit)

    def add(self):
        self.step += 1
        steps = len(self.bits)
        got = self.order(self.got)
        if self.step < steps:
            self.kept, self.sent = halve(self.kept, got)
        elif self.step == steps:
            (own,) = halve(self.kept, got, 1)
            for bit in range(HALVINGS, bits_of("dp")):
                (own,) = halve(own, swap(own, "dp", bit), 1)
            self.pieces = [own]
            self.sent = own
        else:
            self.pieces.append(got)
            if self.step == 2 * steps:
                return
            self.sent = lay(self.pieces)
        self.order.mark(self.sent)


class Scatter:
    def __init__(self, order, kept, sent, bits):
        self.order, self.kept, self.sent, self.bits, self.step = order, kept, sent, bits, 0

    def send(self):
        inner = bits_of("mp")
        bit = self.bits[self.step]
        axis, bit = ("mp", bit) if bit < inner else ("dp", bit - inner)
        self.got = swap(self.sent, axis, bit)

    def add(self):
        self.step += 1
        got = self.order(self.got)
        if self.step < len(self.bits):
            self.kept, self.sent = halve(self.kept, got)
            self.order.mark(self.sent)
        else:
            (total,) = halve(self.kept, got, 1, F32)
            self.total = self.order.mark(total)[0]

    def finish(self):
        while self.step < len(self.bits):
            self.add()
            if self.step < len(self.bits):
                self.send()


def per_device(
    block_in,
    segment_ids,
    first_gain,
    in_proj,
    conv_kernel,
    out_proj,
    second_gain,
    gate_proj,
    up_proj,
    down_proj,
    out_grad,
):
    rows = block_in.shape[1]
    features = block_in.shape[2]
    x = block_in.reshape(rows, features)
    own_ids = segment_ids.reshape(rows)
    cotangent = out_grad.reshape(rows, features)
    inner = lax.axis_size("mp")
    place = (lax.axis_index("dp") % PARTS).reshape(1).astype(jnp.int32)
    place_all = (lax.axis_index("dp") * inner + lax.axis_index("mp")).reshape(1).astype(jnp.int32)
    order = Order()

    def swap_all(block, bit):
        outer = bit - bits_of("mp")
        return swap(block, "mp", bit) if outer < 0 else swap(block, "dp", outer)

    before = shift(x[rows - RIM :], "mp", 1)
    ids_before = shift(own_ids[rows - RIM :].astype(F32), "mp", 1).astype(jnp.int32)
    ids_before = jnp.where(lax.axis_index("mp") == 0, -1, ids_before)
    ids = jnp.concatenate([ids_before, own_ids], 0)
    skip = RIM - (KERNEL - 1)
    same = [(ids[skip + k : skip + k + rows] == own_ids)[:, None] for k in range(KERNEL)]
    same = jnp.pad(jnp.concatenate(same, 1).astype(F32), ((0, 0), (0, LANES - KERNEL)))

    weight_in = lax.all_gather(in_proj, ("dp", "mp"), axis=0, tiled=True)
    small = jnp.concatenate(
        [first_gain[:, None], second_gain[:, None], conv_kernel], 1
    )
    small = jnp.pad(small, ((0, 0), (0, LANES - small.shape[1])))
    weight_bits = list(reversed(range(bits_of("mp") + bits_of("dp"))))
    gathered = [jnp.concatenate([out_proj, small], 1)[None]]
    for bit in weight_bits:
        held = jnp.concatenate(gathered, 0)
        gathered = [held, swap_all(held, bit)]
    group_grad = gather_mp(cotangent)
    weight_in = after(weight_in, gathered, before, group_grad)

    mixer_all, low_all, gated_low, vec, residual, second_low = mix_front(
        place_all, weight_bits, weight_in, gathered, x, before, same
    )

    hidden_units = gate_proj.shape[1]
    bits_all = list(range(bits_of("mp") + bits_of("dp")))
    beside = swap(second_low, "mp", 0)
    across = swap(second_low, "mp", 1)
    *near_acts, og, ou, od = near_feed(
        [second_low, beside], group_grad[:2], gate_proj, up_proj, down_proj
    )
    near_grads = [og, ou, od]
    order.mark(near_grads[0])
    across = order(across)
    far = (
        place, [across, swap(across, "mp", 0)], group_grad[2:], gate_proj, up_proj, down_proj,
        near_grads,
    )
    wide = hidden_units // 3
    assert wide % LANES == 0
    far_acts, sums = (), []
    for n in range(3):
        far_acts, [pair] = far_feed(*far, far_acts, [(0, 1, 2)], wide, n)
        order.mark(pair[1])
        sums.append(Sum(order, *pair, (0, 1, 2)))
        if n == 0:
            sums[0].send()
    one, two, three = sums

    def back(acts, n):
        gate_low, up_low = order((acts[2 + n], acts[4 + n]))
        grad = dot(gate_low, gate_proj, NT) + dot(up_low, up_proj, NT)
        return order.mark(grad.astype(BF16))

    def onward(acts, n):
        return order.mark(dot(order(acts[n]), down_proj, NN).astype(BF16))

    def both(kept, got):
        (total,) = halve(kept[None], order(got)[None], 1)
        return order.mark(total)[0]

    got = swap(back(far_acts, 1), "mp", 0)
    one.add()
    one.send()
    two.send()
    back_across = swap(both(back(far_acts, 0), got), "mp", 1)
    back_beside = swap(back(near_acts, 1), "mp", 0)
    one.add()
    one.send()
    back_near = back(near_acts, 0)
    two.add()
    two.send()
    three.send()
    one.add()
    one.send()

    back_across, back_beside = order((back_across, back_beside))
    residual_grad, residual_low, closing_low, product_part, rim_out, totals = mix_back(
        place_all, weight_bits, back_near, back_beside, back_across, cotangent, residual,
        mixer_all, gathered, vec, same,
    )
    order.mark(rim_out)
    rim_back = shift(rim_out, "mp", -1)
    one.add()
    one.send()
    two.add()
    two.send()
    halves = mix_outer(
        place_all, bits_all, gated_low, order(residual_low), low_all, closing_low, totals
    )
    order.mark(halves[1])
    outer = Scatter(order, *halves, bits_all)
    outer.send()
    three.add()
    three.send()
    outer.add()
    outer.send()
    one.add()
    one.send()
    first_part, last_part, *halves = mix_grads(
        place_all, bits_all, product_part, order(rim_back), mixer_all, low_all
    )
    order.mark(halves[1])
    rest = Scatter(order, *halves, bits_all)
    rest.send()
    two.add()
    two.send()
    rest.add()
    rest.send()
    three.add()
    three.send()
    input_grad = input_back(
        order(first_part), closing_low, last_part, weight_in, residual_grad, x, vec,
    )
    order.mark(input_grad)
    input_grad = input_grad.reshape(1, rows, features)
    two.add()
    two.send()
    three.add()
    three.send()
    outer.add()
    outer.send()
    one.add()
    got = swap(onward(far_acts, 1), "mp", 0)
    two.add()
    two.send()
    three.add()
    three.send()
    on_far = both(onward(far_acts, 0), got)
    rest.add()
    rest.send()
    outer.add()
    outer.send()
    three.add()
    three.send()
    on_across = swap(order(on_far), "mp", 1)
    on_beside = swap(onward(near_acts, 1), "mp", 0)
    on_near = onward(near_acts, 0)
    rest.add()
    rest.send()
    outer.add()
    outer.send()
    done = unpack(place, one.pieces, (), one.bits, wide, 0, features, hidden_units)
    order.mark(done[0])
    rest.add()
    rest.send()
    outer.finish()
    two.add()
    done = unpack(place, two.pieces, done, two.bits, wide, 1, features, hidden_units)
    order.mark(done[0])
    rest.finish()
    branch = on_near.astype(F32) + on_beside.astype(F32) + order(on_across).astype(F32)
    layer_out = order.mark((residual + branch).astype(BF16)).reshape(1, rows, features)
    grad_out = outer.total[:, :features]
    grad_second = outer.total[:, features]
    grad_conv = outer.total[:, features + 1 : features + 1 + KERNEL]
    ends = rest.total
    grad_in = jnp.concatenate(
        [ends[:, :features], outer.total[:, features + LANES :], ends[:, features:]], 1
    )
    grad_first = jnp.sum(grad_in * in_proj.astype(F32), axis=1) / first_gain.astype(F32)
    three.add()
    grad_gate, grad_up, grad_down = unpack(
        place, three.pieces, done, three.bits, wide, 2, features, hidden_units
    )
    return (
        layer_out,
        input_grad,
        grad_first,
        grad_in,
        grad_conv,
        grad_out,
        grad_second,
        grad_gate,
        grad_up,
        grad_down,
    )


def solution(mesh):
    in_specs = (
        P("dp", "mp", None),
        P("dp", "mp"),
        P(("dp", "mp")),
        P(("dp", "mp"), None),
        P(("dp", "mp"), None),
        P(("dp", "mp"), None),
        P(("dp", "mp")),
        P(None, "mp"),
        P(None, "mp"),
        P("mp", None),
        P("dp", "mp", None),
    )
    out_specs = (
        P("dp", "mp", None),
        P("dp", "mp", None),
        P(("dp", "mp")),
        P(("dp", "mp"), None),
        P(("dp", "mp"), None),
        P(("dp", "mp"), None),
        P(("dp", "mp")),
        P(None, "mp"),
        P(None, "mp"),
        P("mp", None),
    )
    return jax.shard_map(
        per_device, mesh=mesh, in_specs=in_specs, out_specs=out_specs, check_vma=False
    )
```

```python
import functools

import jax
import jax.numpy as jnp
from jax import lax
from jax.experimental import pallas as pl
from jax.experimental.pallas import tpu as pltpu
from jax.sharding import PartitionSpec as P

KERNEL = 3
LANES = 128
BF16 = jnp.bfloat16
F32 = jnp.float32
HALVINGS = 3
PARTS = 1 << HALVINGS
NN = (((1,), (0,)), ((), ()))
NT = (((1,), (1,)), ((), ()))
TN = (((0,), (0,)), ((), ()))
VMEM_LIMIT = 60 * 1024 * 1024
LONG = pl.CostEstimate(flops=10**11, transcendentals=0, bytes_accessed=0)

epsilon = 1e-05


def swap(block, axis, bit):
    size = lax.axis_size(axis)
    return lax.ppermute(block, axis, [(i, i ^ (1 << bit)) for i in range(size)])


def shift(block, axis, distance):
    devices = range(lax.axis_size(axis))
    route = [(i - distance, i) for i in devices if i - distance in devices]
    return lax.ppermute(block, axis, route)


def bit_of(axis, bit):
    return (lax.axis_index(axis) >> bit) & 1


def bits_of(axis):
    size = lax.axis_size(axis)
    assert size & (size - 1) == 0
    return size.bit_length() - 1


def after(values, *before):
    return lax.optimization_barrier((values, before))[0]


class Order:
    def __init__(self):
        self.last = ()

    def __call__(self, values):
        return after(values, self.last)

    def mark(self, out):
        self.last = out
        return out


def away(bits):
    top = len(bits) - 1
    return [sum(((q >> (top - n)) & 1) << bit for n, bit in enumerate(bits)) for q in range(PARTS)]


def dot(left, right, dims):
    return lax.dot_general(left, right, dims, preferred_element_type=F32)


def activate(gate_val, up_val, hidden_grad):
    sig = 1.0 / (1.0 + jnp.exp(-gate_val))
    silu = gate_val * sig
    return (
        (silu * up_val).astype(BF16),
        (hidden_grad * up_val * (sig * (1.0 + gate_val * (1.0 - sig)))).astype(BF16),
        (hidden_grad * silu).astype(BF16),
    )


def feed(x_ref, go_ref, gate_ref, up_ref, down_ref, acts, outs):
    for n in range(2):
        step = x_ref.shape[0] // 2
        part = slice(n * step, (n + 1) * step)
        gate_val = dot(x_ref[part], gate_ref[...], NN)
        up_val = dot(x_ref[part], up_ref[...], NN)
        hidden_grad = dot(go_ref[part], down_ref[...], NT)
        for m, value in enumerate(activate(gate_val, up_val, hidden_grad)):
            acts[m][part] = value
            outs[2 * m + n][...] = value


def join(first, xa_ref, xb_ref, ga_ref, gb_ref, x_ref, go_ref):
    rows = xa_ref.shape[0]

    @pl.when(first)
    def _():
        x_ref[:rows] = xa_ref[...]
        x_ref[rows:] = xb_ref[...]
        go_ref[:rows] = ga_ref[...]
        go_ref[rows:] = gb_ref[...]


def near_kernel(xa_ref, xb_ref, ga_ref, gb_ref, gate_ref, up_ref, down_ref,
                *refs):
    outs = refs[:6]
    og_ref, ou_ref, od_ref, x_ref, go_ref, hid_ref, gl_ref, ul_ref = refs[6:]
    join(pl.program_id(0) == 0, xa_ref, xb_ref, ga_ref, gb_ref, x_ref, go_ref)
    feed(x_ref, go_ref, gate_ref, up_ref, down_ref, (hid_ref, gl_ref, ul_ref), outs)
    og_ref[...] = dot(x_ref[...], gl_ref[...], TN).astype(BF16)
    ou_ref[...] = dot(x_ref[...], ul_ref[...], TN).astype(BF16)
    od_ref[...] = dot(hid_ref[...], go_ref[...], TN).astype(BF16)


def near_feed(xs, gos, gate, up, down):
    rows, features = xs[0].shape
    hidden = gate.shape[1]
    wide = 256
    tokens = 2 * rows
    whole = pl.BlockSpec((rows, features), lambda i: (0, 0), pipeline_mode=pl.Buffered(1))
    col = pl.BlockSpec((features, wide), lambda i: (0, i))
    row = pl.BlockSpec((wide, features), lambda i: (i, 0))
    act = pl.BlockSpec((rows, wide), lambda i: (0, i))
    return pl.pallas_call(
        near_kernel,
        grid=(pl.cdiv(hidden, wide),),
        in_specs=[whole] * 4 + [col, col, row],
        out_specs=[act] * 6 + [col, col, row],
        out_shape=[jax.ShapeDtypeStruct((rows, hidden), BF16)] * 6
        + [jax.ShapeDtypeStruct((features, hidden), BF16)] * 2
        + [jax.ShapeDtypeStruct((hidden, features), BF16)],
        scratch_shapes=[pltpu.VMEM((tokens, features), BF16)] * 2
        + [pltpu.VMEM((tokens, wide), BF16)] * 3,
        compiler_params=pltpu.CompilerParams(vmem_limit_bytes=VMEM_LIMIT),
        cost_estimate=LONG,
        name="near_feed",
    )(*xs, *gos, gate, up, down)


def far_kernel(orders, place_ref, xa_ref, xb_ref, ga_ref, gb_ref, gate_ref, up_ref, down_ref,
               ng_ref, nu_ref, nd_ref, *refs):
    blocks = len(orders)
    x_ref, go_ref, tg_ref, tu_ref, td_ref, hid_ref, gl_ref, ul_ref = refs[-8:]
    packs = refs[-8 - 2 * blocks : -8]
    outs = refs[-14 - 2 * blocks : -8 - 2 * blocks]
    now = pl.program_id(0)
    join(now == 0, xa_ref, xb_ref, ga_ref, gb_ref, x_ref, go_ref)
    feed(x_ref, go_ref, gate_ref, up_ref, down_ref, (hid_ref, gl_ref, ul_ref), outs)
    tg_ref[...] = ng_ref[...].astype(F32) + dot(x_ref[...], gl_ref[...], TN)
    tu_ref[...] = nu_ref[...].astype(F32) + dot(x_ref[...], ul_ref[...], TN)
    td_ref[...] = nd_ref[...].astype(F32) + dot(hid_ref[...], go_ref[...], TN)
    features, wide = tg_ref.shape
    tall, low = features // PARTS, wide // PARTS
    for n, bits in enumerate(orders):

        @pl.when(now == n)
        def _(n=n, bits=bits):
            for q, far in enumerate(away(bits or (0, 1, 2))):
                part = place_ref[0] ^ far if bits else far
                half = PARTS // 2
                out = packs[2 * n + q // half].at[q % half]
                rows = pl.ds(part * tall, tall)
                at = 0
                for grad_ref in (tg_ref, tu_ref):
                    for c in range(0, wide, LANES):
                        out[at : at + tall] = grad_ref[rows, c : c + LANES].astype(BF16)
                        at += tall
                rows = pl.ds(part * low, low)
                for c in range(0, features, LANES):
                    out[at : at + low] = td_ref[rows, c : c + LANES].astype(BF16)
                    at += low


def far_feed(place, xs, gos, gate, up, down, near_grads, before, orders, wide, index):
    rows, features = xs[0].shape
    tokens = 2 * rows
    hidden = gate.shape[1]
    blocks = len(orders)
    whole = pl.BlockSpec((rows, features), lambda i, _: (0, 0), pipeline_mode=pl.Buffered(1))
    col = pl.BlockSpec((features, wide), lambda i, _: (0, index + i))
    row = pl.BlockSpec((wide, features), lambda i, _: (index + i, 0))
    act = pl.BlockSpec((rows, wide), lambda i, _: (0, index + i))
    packed = 3 * features * wide // PARTS // LANES
    half = pl.BlockSpec((PARTS // 2, packed, LANES), lambda i, _: (0, 0, 0), pipeline_mode=pl.Buffered(1))
    first = 1 + 4 + 3 + 3
    results = pl.pallas_call(
        functools.partial(far_kernel, orders),
        grid_spec=pltpu.PrefetchScalarGridSpec(
            num_scalar_prefetch=1,
            grid=(blocks,),
            in_specs=[whole] * 4
            + [col, col, row] * 2
            + [pl.BlockSpec(memory_space=pl.ANY)] * len(before),
            out_specs=[act] * 6 + [half] * (2 * blocks),
            scratch_shapes=[pltpu.VMEM((tokens, features), BF16)] * 2
            + [pltpu.VMEM((features, wide), F32)] * 2
            + [pltpu.VMEM((wide, features), F32)]
            + [pltpu.VMEM((tokens, wide), BF16)] * 3,
        ),
        out_shape=[jax.ShapeDtypeStruct((rows, hidden), BF16)] * 6
        + [jax.ShapeDtypeStruct((PARTS // 2, packed, LANES), BF16)] * (2 * blocks),
        input_output_aliases={first + n: n for n in range(len(before))},
        compiler_params=pltpu.CompilerParams(vmem_limit_bytes=VMEM_LIMIT),
        cost_estimate=LONG,
        name="far_feed",
    )(place, *xs, *gos, gate, up, down, *near_grads, *before)
    return results[:6], list(zip(results[6::2], results[7::2]))


def unpack_kernel(bits, pieces, place_ref, *refs):
    og_ref, ou_ref, od_ref = refs[-3:]
    features, wide = og_ref.shape
    tall, low = features // PARTS, wide // PARTS
    sources = [ref.at[n] for ref in refs[:pieces] for n in range(ref.shape[0])]
    for source, far in zip(sources, away(bits or (0, 1, 2))):
        part = place_ref[0] ^ far if bits else far
        rows = pl.ds(part * tall, tall)
        at = 0
        for out in (og_ref, ou_ref):
            for c in range(0, wide, LANES):
                out[rows, c : c + LANES] = source[at : at + tall].astype(F32)
                at += tall
        rows = pl.ds(part * low, low)
        for c in range(0, features, LANES):
            od_ref[rows, c : c + LANES] = source[at : at + low].astype(F32)
            at += low


def unpack(place, pieces, before, bits, wide, index, features, hidden):
    packed = pieces[0].shape[1]
    ins = [
        pl.BlockSpec((piece.shape[0], packed, LANES), lambda i, _: (0, 0, 0)) for piece in pieces
    ]
    col = pl.BlockSpec((features, wide), lambda i, _: (0, index))
    row = pl.BlockSpec((wide, features), lambda i, _: (index, 0))
    keep = [pl.BlockSpec(memory_space=pl.ANY)] * len(before)
    return pl.pallas_call(
        functools.partial(unpack_kernel, bits, len(pieces)),
        grid_spec=pltpu.PrefetchScalarGridSpec(
            num_scalar_prefetch=1,
            grid=(1,),
            in_specs=ins + keep,
            out_specs=[col, col, row],
        ),
        out_shape=[jax.ShapeDtypeStruct((features, hidden), F32)] * 2
        + [jax.ShapeDtypeStruct((hidden, features), F32)],
        input_output_aliases={1 + len(ins) + n: n for n in range(len(before))},
        compiler_params=pltpu.CompilerParams(vmem_limit_bytes=VMEM_LIMIT),
        cost_estimate=LONG,
        name="unpack",
    )(place, *pieces, *before)


def add_low(one, two):
    return (one.astype(F32) + two.astype(F32)).astype(BF16)


def whole(array):
    return pl.BlockSpec(array.shape, lambda i: (0,) * array.ndim)


def halve_kernel(kept_ref, got_ref, *outs):
    half = outs[-1].shape[0]
    for n, out in enumerate(outs):
        part = slice(n * half, (n + 1) * half)
        out[...] = (kept_ref[part].astype(F32) + got_ref[part].astype(F32)).astype(out.dtype)


def halve(kept, got, halves=2, dtype=BF16):
    count, tall, wide = kept.shape
    shapes = [jax.ShapeDtypeStruct((count // halves, tall, wide), dtype)] * halves
    return pl.pallas_call(
        halve_kernel,
        grid=(1,),
        in_specs=[whole(kept), whole(got)],
        out_specs=[whole(s) for s in shapes],
        out_shape=shapes,
        compiler_params=pltpu.CompilerParams(vmem_limit_bytes=VMEM_LIMIT),
        cost_estimate=LONG,
        name="halve",
    )(kept, got)


def lay_kernel(*refs):
    at = 0
    for ref in refs[:-1]:
        refs[-1][at : at + ref.shape[0]] = ref[...]
        at += ref.shape[0]


def lay(pieces):
    _, tall, wide = pieces[0].shape
    shape = jax.ShapeDtypeStruct((sum(p.shape[0] for p in pieces), tall, wide), pieces[0].dtype)
    return pl.pallas_call(
        lay_kernel,
        grid=(1,),
        in_specs=[whole(p) for p in pieces],
        out_specs=whole(shape),
        out_shape=shape,
        compiler_params=pltpu.CompilerParams(vmem_limit_bytes=VMEM_LIMIT),
        cost_estimate=LONG,
        name="lay",
    )(*pieces)


def pack_rows(place, bits, grad_ref, kept_ref, sent_ref, lane):
    count = len(bits)
    half, tall, _ = kept_ref.shape
    wide = grad_ref.shape[1]

    def move(q, out_ref, slot):
        far = 0
        for n, bit in enumerate(bits):
            far = far | (((q >> (count - 1 - n)) & 1) << bit)
        rows = pl.ds(pl.multiple_of((place ^ far) * tall, tall), tall)
        out_ref[slot, :, lane : lane + wide] = grad_ref[rows].astype(BF16)

    @pl.loop(0, half)
    def _(q):
        move(q, kept_ref, q)
        move(q + half, sent_ref, q)


STRIP = 64
RIM = 8


def fold(values):
    return jnp.sum(values.reshape(values.shape[0] // 8, 8, values.shape[1]), axis=0)


def assemble(place, bits, sources, width, target_ref, lane, sems):
    half, tall, _ = sources[0][0].shape
    count = len(bits)

    def copy(q, n):
        ref, start = sources[n]
        far = 0
        for m, bit in enumerate(bits):
            far = far | ((((q + n * half) >> m) & 1) << bit)
        rows = pl.ds(pl.multiple_of((place ^ far) * tall, tall), tall)
        return pltpu.make_async_copy(
            ref.at[q, :, start : start + width],
            target_ref.at[rows, lane : lane + width],
            sems.at[n * half + q],
        )

    @pl.loop(0, half)
    def _(q):
        for n in range(2):
            copy(q, n).start()

    def wait():
        @pl.loop(0, half)
        def _(q):
            for n in range(2):
                copy(q, n).wait()

    return wait


def mix_front_kernel(bits, place_ref, in_any, c0, c1, x_ref, before_ref, same_ref,
                     mix_any, low_any, gated_any, vec_ref, res_ref, second_ref,
                     w_ref, wo_ref, mix_ref, low_ref, gated_ref, ext_ref, sems, in_sem, out_sem):
    place = place_ref[0]
    rows, features = x_ref.shape
    last = features + LANES
    wide = features
    loads = [
        pltpu.make_async_copy(
            in_any.at[:, n * wide : (n + 1) * wide], w_ref.at[:, n * wide : (n + 1) * wide], in_sem.at[n]
        )
        for n in range(3)
    ]
    wait_out = assemble(place, bits, [(c0, 0), (c1, 0)], features + LANES, wo_ref, 0, sems)
    for load in loads:
        load.start()
    wait_out()
    vec_ref[...] = wo_ref[:, features:].astype(F32).T[:8]
    gain_one, gain_two = vec_ref[0:1], vec_ref[1:2]
    taps = [vec_ref[2 + k : 3 + k] for k in range(KERNEL)]

    def normed(values, gain):
        inverse = lax.rsqrt(jnp.mean(values * values, axis=-1, keepdims=True) + epsilon)
        return (values * inverse * gain).astype(BF16)

    low_ref[:RIM] = normed(before_ref[...].astype(F32), gain_one)

    @pl.loop(0, rows // STRIP)
    def _(i):
        at = pl.ds(pl.multiple_of(i * STRIP, STRIP), STRIP)
        inner = pl.ds(pl.multiple_of(i * STRIP + RIM, RIM), STRIP)
        low_ref[inner] = normed(x_ref[at].astype(F32), gain_one)

    stores = [pltpu.make_async_copy(low_ref, low_any, out_sem.at[0])]
    stores[0].start()
    for n, load in enumerate(loads):
        load.wait()
        part = slice(n * wide, (n + 1) * wide)
        mix_ref[:, part] = dot(low_ref[...], w_ref[:, part], NN)
        stores.append(
            pltpu.make_async_copy(mix_ref.at[:, part], mix_any.at[:, part], out_sem.at[1 + n])
        )
        stores[-1].start()
    ext_ref[:RIM] = mix_ref[:RIM, :features] * mix_ref[:RIM, 2 * features :]

    @pl.loop(0, rows // STRIP)
    def _(i):
        at = pl.ds(pl.multiple_of(i * STRIP + RIM, RIM), STRIP)
        ext_ref[at] = mix_ref[at, :features] * mix_ref[at, 2 * features :]

    @pl.loop(0, rows // STRIP)
    def _(i):
        at = pl.ds(pl.multiple_of(i * STRIP, STRIP), STRIP)
        inner = pl.ds(pl.multiple_of(i * STRIP + RIM, RIM), STRIP)
        window = ext_ref[pl.ds(pl.multiple_of(i * STRIP, STRIP), STRIP + RIM)]
        skip = RIM - (KERNEL - 1)
        conv = 0.0
        for k in range(KERNEL):
            same = same_ref[at, k : k + 1] > 0.5
            conv += jnp.where(same, window[skip + k : skip + k + STRIP], 0.0) * taps[k]
        gated_ref[at] = (mix_ref[inner, features : 2 * features] * conv).astype(BF16)

    stores.append(pltpu.make_async_copy(gated_ref, gated_any, out_sem.at[4]))
    stores[-1].start()
    res_ref[...] = dot(gated_ref[...], wo_ref[:, :features], NN)

    @pl.loop(0, rows // STRIP)
    def _(i):
        at = pl.ds(pl.multiple_of(i * STRIP, STRIP), STRIP)
        residual = x_ref[at].astype(F32) + res_ref[at]
        res_ref[at] = residual
        second_ref[at] = normed(residual, gain_two)

    for store in stores:
        store.wait()


def mix_front(place, bits, weight_in, gathered, x, before, same):
    rows, features = x.shape
    anywhere = pl.BlockSpec(memory_space=pl.ANY)
    outs = [
        jax.ShapeDtypeStruct((rows + RIM, 3 * features), F32),
        jax.ShapeDtypeStruct((rows + RIM, features), BF16),
        jax.ShapeDtypeStruct((rows, features), BF16),
        jax.ShapeDtypeStruct((8, features), F32),
        jax.ShapeDtypeStruct((rows, features), F32),
        jax.ShapeDtypeStruct((rows, features), BF16),
    ]
    return pl.pallas_call(
        functools.partial(mix_front_kernel, bits),
        grid_spec=pltpu.PrefetchScalarGridSpec(
            num_scalar_prefetch=1,
            grid=(1,),
            in_specs=[anywhere] * 3 + [once(x), once(before), once(same)],
            out_specs=[anywhere] * 3 + [once(s) for s in outs[3:]],
            scratch_shapes=[
                pltpu.VMEM((features, 3 * features), BF16),
                pltpu.VMEM((features, features + LANES), BF16),
                pltpu.VMEM((rows + RIM, 3 * features), F32),
                pltpu.VMEM((rows + RIM, features), BF16),
                pltpu.VMEM((rows, features), BF16),
                pltpu.VMEM((rows + RIM, features), F32),
                pltpu.SemaphoreType.DMA((1 << len(bits),)),
                pltpu.SemaphoreType.DMA((3,)),
                pltpu.SemaphoreType.DMA((5,)),
            ],
        ),
        out_shape=outs,
        compiler_params=pltpu.CompilerParams(vmem_limit_bytes=VMEM_LIMIT),
        cost_estimate=LONG,
        name="mix_front",
    )(place, weight_in, *gathered, x, before, same)


def onward_kernel(place_ref, *refs):
    *hids, down_ref, out_ref = refs
    for n, hid_ref in enumerate(hids):

        @pl.when(pl.program_id(0) == n)
        def _(hid_ref=hid_ref):
            out_ref[...] = dot(hid_ref[...], down_ref[...], NN).astype(BF16)


def onward(place, hids, down):
    rows, hidden = hids[0].shape
    features = down.shape[1]
    return pl.pallas_call(
        onward_kernel,
        grid_spec=pltpu.PrefetchScalarGridSpec(
            num_scalar_prefetch=1,
            grid=(len(hids),),
            in_specs=[once(a) for a in (*hids, down)],
            out_specs=pl.BlockSpec((rows, features), lambda i, place: (place[0] ^ i, 0)),
        ),
        out_shape=jax.ShapeDtypeStruct((len(hids) * rows, features), BF16),
        compiler_params=pltpu.CompilerParams(vmem_limit_bytes=VMEM_LIMIT),
        cost_estimate=LONG,
        name="onward",
    )(place, *hids, down)


def mix_back_kernel(bits, place_ref, near_ref, beside_ref, across_ref, cot_ref, res_ref, mix_ref,
                    c0, c1, vec_ref, same_ref,
                    rg_ref, rlow_ref, cl_ref, pg_ref, rim_ref, sums_ref,
                    ext_ref, gg_ref, d0_ref, d1_ref, d2_ref, w_ref, sems):
    rows, features = res_ref.shape
    wait = assemble(place_ref[0], bits, [(c0, 0), (c1, 0)], features, w_ref, 0, sems)
    sums_ref[...] = jnp.zeros_like(sums_ref)
    gain = vec_ref[1:2]
    taps = [vec_ref[2 + k : 3 + k] for k in range(KERNEL)]

    @pl.loop(0, rows // STRIP)
    def _(i):
        at = pl.ds(pl.multiple_of(i * STRIP, STRIP), STRIP)
        second = near_ref[at].astype(F32) + beside_ref[at].astype(F32) + across_ref[at].astype(F32)
        residual = res_ref[at]
        inverse = lax.rsqrt(jnp.mean(residual * residual, axis=-1, keepdims=True) + epsilon)
        unit = residual * inverse
        weighted = second * gain
        mean = jnp.mean(weighted * unit, axis=-1, keepdims=True)
        grad = cot_ref[at].astype(F32) + inverse * (weighted - unit * mean)
        rg_ref[at] = grad
        rlow_ref[at] = grad.astype(BF16)
        sums_ref[0] += fold(second * unit)

    wait()
    gg_ref[...] = dot(rlow_ref[...], w_ref[...], NT)
    ext_ref[:RIM] = mix_ref[:RIM, :features] * mix_ref[:RIM, 2 * features :]

    @pl.loop(0, rows // STRIP)
    def _(i):
        at = pl.ds(pl.multiple_of(i * STRIP + RIM, RIM), STRIP)
        ext_ref[at] = mix_ref[at, :features] * mix_ref[at, 2 * features :]

    zeros = jnp.zeros((RIM, features), F32)
    for d_ref in (d0_ref, d1_ref, d2_ref):
        d_ref[:RIM] = zeros
        d_ref[rows + RIM :] = zeros

    @pl.loop(0, rows // STRIP)
    def _(i):
        at = pl.ds(pl.multiple_of(i * STRIP, STRIP), STRIP)
        inner = pl.ds(pl.multiple_of(i * STRIP + RIM, RIM), STRIP)
        window = ext_ref[pl.ds(pl.multiple_of(i * STRIP, STRIP), STRIP + RIM)]
        skip = RIM - (KERNEL - 1)
        same = [same_ref[at, k : k + 1] > 0.5 for k in range(KERNEL)]
        past = [
            jnp.where(same[k], window[skip + k : skip + k + STRIP], 0.0) for k in range(KERNEL)
        ]
        conv = past[0] * taps[0] + past[1] * taps[1] + past[2] * taps[2]
        gated_grad = gg_ref[at]
        cl_ref[at] = (gated_grad * conv).astype(BF16)
        conv_grad = gated_grad * mix_ref[inner, features : 2 * features]
        for k, d_ref in enumerate((d0_ref, d1_ref, d2_ref)):
            sums_ref[1 + k] += fold(conv_grad * past[k])
            d_ref[inner] = jnp.where(same[k], conv_grad * taps[k], 0.0)

    rim_ref[...] = d0_ref[2 : 2 + RIM] + d1_ref[1 : 1 + RIM]

    @pl.loop(0, rows // STRIP)
    def _(i):
        at = pl.ds(pl.multiple_of(i * STRIP, STRIP), STRIP)
        window = pl.ds(pl.multiple_of(i * STRIP + RIM, RIM), STRIP + RIM)
        inner = pl.ds(pl.multiple_of(i * STRIP + RIM, RIM), STRIP)
        pg_ref[at] = (
            d2_ref[inner] + d1_ref[window][1 : 1 + STRIP] + d0_ref[window][2 : 2 + STRIP]
        )


def mix_outer_kernel(bits, place_ref, gated_ref, rlow_ref, low_ref, cl_ref, sums_ref,
                     out_kept, out_sent, acc_ref):
    place = place_ref[0]
    features = acc_ref.shape[0]
    acc_ref[...] = dot(gated_ref[...], rlow_ref[...], TN)
    pack_rows(place, bits, acc_ref, out_kept, out_sent, 0)
    totals = jnp.sum(sums_ref[...], axis=1)
    totals = jnp.concatenate([totals, jnp.zeros_like(totals)], 0)[:8].astype(BF16)
    units = lax.broadcasted_iota(jnp.int32, (8, LANES), 0) == lax.broadcasted_iota(
        jnp.int32, (8, LANES), 1
    )
    acc_ref[:, :LANES] = dot(totals, jnp.where(units, 1.0, 0.0).astype(BF16), TN)
    pack_rows(place, bits, acc_ref.at[:, :LANES], out_kept, out_sent, features)
    acc_ref[...] = dot(low_ref[RIM:], cl_ref[...], TN)
    pack_rows(place, bits, acc_ref, out_kept, out_sent, features + LANES)


def once(array):
    return pl.BlockSpec(array.shape, lambda *_: (0,) * array.ndim, pipeline_mode=pl.Buffered(1))


def mix_back(place, bits, near, beside, across, cot, res, mix, gathered, vec, same):
    rows, features = res.shape
    shapes = [
        jax.ShapeDtypeStruct((rows, features), F32),
        jax.ShapeDtypeStruct((rows, features), BF16),
        jax.ShapeDtypeStruct((rows, features), BF16),
        jax.ShapeDtypeStruct((rows, features), F32),
        jax.ShapeDtypeStruct((RIM, features), F32),
        jax.ShapeDtypeStruct((1 + KERNEL, 8, features), F32),
    ]
    ins = [near, beside, across, cot, res, mix]
    anywhere = pl.BlockSpec(memory_space=pl.ANY)
    return pl.pallas_call(
        functools.partial(mix_back_kernel, bits),
        grid_spec=pltpu.PrefetchScalarGridSpec(
            num_scalar_prefetch=1,
            grid=(1,),
            in_specs=[once(a) for a in ins] + [anywhere] * 2 + [once(vec), once(same)],
            out_specs=[once(s) for s in shapes],
            scratch_shapes=[
                pltpu.VMEM((rows + RIM, features), F32),
                pltpu.VMEM((rows, features), F32),
                *[pltpu.VMEM((rows + 2 * RIM, features), F32)] * 3,
                pltpu.VMEM((features, features), BF16),
                pltpu.SemaphoreType.DMA((1 << len(bits),)),
            ],
        ),
        out_shape=shapes,
        compiler_params=pltpu.CompilerParams(vmem_limit_bytes=VMEM_LIMIT),
        cost_estimate=LONG,
        name="mix_back",
    )(place, *ins, *gathered, vec, same)


def mix_outer(place, bits, gated, rlow, low, cl, sums):
    features = gated.shape[1]
    parts = 1 << len(bits)
    ins = [gated, rlow, low, cl, sums]
    shapes = [
        jax.ShapeDtypeStruct((parts // 2, features // parts, 2 * features + LANES), BF16)
    ] * 2
    return pl.pallas_call(
        functools.partial(mix_outer_kernel, bits),
        grid_spec=pltpu.PrefetchScalarGridSpec(
            num_scalar_prefetch=1,
            grid=(1,),
            in_specs=[once(a) for a in ins],
            out_specs=[once(s) for s in shapes],
            scratch_shapes=[pltpu.VMEM((features, features), F32)],
        ),
        out_shape=shapes,
        compiler_params=pltpu.CompilerParams(vmem_limit_bytes=VMEM_LIMIT),
        cost_estimate=LONG,
        name="mix_outer",
    )(place, *ins)


def mix_grads_kernel(bits, place_ref, pg_ref, rim_ref, mix_ref, low_ref,
                     first_ref, last_ref, kept_ref, sent_ref, acc_ref):
    place = place_ref[0]
    rows, features = pg_ref.shape

    @pl.loop(0, rows // STRIP)
    def _(i):
        at = pl.ds(pl.multiple_of(i * STRIP, STRIP), STRIP)
        inner = pl.ds(pl.multiple_of(i * STRIP + RIM, RIM), STRIP)
        grad = pg_ref[at]
        first_ref[at] = (grad * mix_ref[inner, 2 * features :]).astype(BF16)
        last_ref[at] = (grad * mix_ref[inner, :features]).astype(BF16)

    grad = pg_ref[rows - RIM :] + rim_ref[...]
    first_ref[rows - RIM :] = (grad * mix_ref[rows:, 2 * features :]).astype(BF16)
    last_ref[rows - RIM :] = (grad * mix_ref[rows:, :features]).astype(BF16)
    for n, grad_ref in enumerate((first_ref, last_ref)):
        acc_ref[...] = dot(low_ref[RIM:], grad_ref[...], TN)
        pack_rows(place, bits, acc_ref, kept_ref, sent_ref, n * features)


def mix_grads(place, bits, pg, rim, mix, low):
    rows, features = pg.shape
    parts = 1 << len(bits)
    tall = features // parts

    def whole(array):
        return pl.BlockSpec(
            array.shape, lambda i, _: (0,) * array.ndim, pipeline_mode=pl.Buffered(1)
        )

    shapes = [jax.ShapeDtypeStruct((rows, features), BF16)] * 2
    shapes += [jax.ShapeDtypeStruct((parts // 2, tall, 2 * features), BF16)] * 2
    return pl.pallas_call(
        functools.partial(mix_grads_kernel, bits),
        grid_spec=pltpu.PrefetchScalarGridSpec(
            num_scalar_prefetch=1,
            grid=(1,),
            in_specs=[whole(a) for a in (pg, rim, mix, low)],
            out_specs=[whole(s) for s in shapes],
            scratch_shapes=[pltpu.VMEM((features, features), F32)],
        ),
        out_shape=shapes,
        compiler_params=pltpu.CompilerParams(vmem_limit_bytes=VMEM_LIMIT),
        cost_estimate=LONG,
        name="mix_grads",
    )(place, pg, rim, mix, low)


def input_back_kernel(first_ref, mid_ref, last_ref, w_ref, rg_ref, x_ref, vec_ref, out_ref, fg_ref):
    rows, features = rg_ref.shape
    fg_ref[...] = dot(first_ref[...], w_ref[:, :features], NT)
    fg_ref[...] += dot(mid_ref[...], w_ref[:, features : 2 * features], NT)
    fg_ref[...] += dot(last_ref[...], w_ref[:, 2 * features :], NT)

    @pl.loop(0, rows // STRIP)
    def _(i):
        at = pl.ds(pl.multiple_of(i * STRIP, STRIP), STRIP)
        values = x_ref[at].astype(F32)
        inverse = lax.rsqrt(jnp.mean(values * values, axis=-1, keepdims=True) + epsilon)
        unit = values * inverse
        weighted = fg_ref[at] * vec_ref[0:1]
        mean = jnp.mean(weighted * unit, axis=-1, keepdims=True)
        out_ref[at] = rg_ref[at] + inverse * (weighted - unit * mean)


def input_back(first, mid, last, weight_in, rg, x, vec):
    rows, features = rg.shape
    ins = [first, mid, last, weight_in, rg, x, vec]
    return pl.pallas_call(
        input_back_kernel,
        grid=(1,),
        in_specs=[once(a) for a in ins],
        out_specs=once(rg),
        out_shape=jax.ShapeDtypeStruct((rows, features), F32),
        scratch_shapes=[pltpu.VMEM((rows, features), F32)],
        compiler_params=pltpu.CompilerParams(vmem_limit_bytes=VMEM_LIMIT),
        cost_estimate=LONG,
        name="input_back",
    )(*ins)


def gather_mp(own):
    size = lax.axis_size("mp")
    blocks = [own] + [None] * (size - 1)
    for bit in reversed(range(bits_of("mp"))):
        for r in [r for r in range(size) if blocks[r] is not None]:
            blocks[r ^ (1 << bit)] = swap(blocks[r], "mp", bit)
    return blocks


class Sum:
    def __init__(self, order, kept, sent, bits):
        self.order, self.kept, self.sent, self.bits, self.step = order, kept, sent, bits, 0

    def send(self):
        steps = len(self.bits)
        bit = self.bits[self.step] if self.step < steps else self.bits[2 * steps - 1 - self.step]
        self.got = swap(self.sent, "dp", bit)

    def add(self):
        self.step += 1
        steps = len(self.bits)
        got = self.order(self.got)
        if self.step < steps:
            self.kept, self.sent = halve(self.kept, got)
        elif self.step == steps:
            (own,) = halve(self.kept, got, 1)
            for bit in range(HALVINGS, bits_of("dp")):
                (own,) = halve(own, swap(own, "dp", bit), 1)
            self.pieces = [own]
            self.sent = own
        else:
            self.pieces.append(got)
            if self.step == 2 * steps:
                return
            self.sent = lay(self.pieces)
        self.order.mark(self.sent)


class Scatter:
    def __init__(self, order, kept, sent, bits):
        self.order, self.kept, self.sent, self.bits, self.step = order, kept, sent, bits, 0

    def send(self):
        inner = bits_of("mp")
        bit = self.bits[self.step]
        axis, bit = ("mp", bit) if bit < inner else ("dp", bit - inner)
        self.got = swap(self.sent, axis, bit)

    def add(self):
        self.step += 1
        got = self.order(self.got)
        if self.step < len(self.bits):
            self.kept, self.sent = halve(self.kept, got)
            self.order.mark(self.sent)
        else:
            (total,) = halve(self.kept, got, 1, F32)
            self.total = self.order.mark(total)[0]

    def finish(self):
        while self.step < len(self.bits):
            self.add()
            if self.step < len(self.bits):
                self.send()


def per_device(
    block_in,
    segment_ids,
    first_gain,
    in_proj,
    conv_kernel,
    out_proj,
    second_gain,
    gate_proj,
    up_proj,
    down_proj,
    out_grad,
):
    rows = block_in.shape[1]
    features = block_in.shape[2]
    x = block_in.reshape(rows, features)
    own_ids = segment_ids.reshape(rows)
    cotangent = out_grad.reshape(rows, features)
    inner = lax.axis_size("mp")
    place = (lax.axis_index("dp") % PARTS).reshape(1).astype(jnp.int32)
    place_all = (lax.axis_index("dp") * inner + lax.axis_index("mp")).reshape(1).astype(jnp.int32)
    order = Order()

    def swap_all(block, bit):
        outer = bit - bits_of("mp")
        return swap(block, "mp", bit) if outer < 0 else swap(block, "dp", outer)

    before = shift(x[rows - RIM :], "mp", 1)
    ids_before = shift(own_ids[rows - RIM :].astype(F32), "mp", 1).astype(jnp.int32)
    ids_before = jnp.where(lax.axis_index("mp") == 0, -1, ids_before)
    ids = jnp.concatenate([ids_before, own_ids], 0)
    skip = RIM - (KERNEL - 1)
    same = [(ids[skip + k : skip + k + rows] == own_ids)[:, None] for k in range(KERNEL)]
    same = jnp.pad(jnp.concatenate(same, 1).astype(F32), ((0, 0), (0, LANES - KERNEL)))

    weight_in = lax.all_gather(in_proj, ("dp", "mp"), axis=0, tiled=True)
    small = jnp.concatenate(
        [first_gain[:, None], second_gain[:, None], conv_kernel], 1
    )
    small = jnp.pad(small, ((0, 0), (0, LANES - small.shape[1])))
    weight_bits = list(reversed(range(bits_of("mp") + bits_of("dp"))))
    gathered = [jnp.concatenate([out_proj, small], 1)[None]]
    for bit in weight_bits:
        held = jnp.concatenate(gathered, 0)
        gathered = [held, swap_all(held, bit)]
    group_grad = gather_mp(cotangent)
    weight_in = after(weight_in, gathered, before, group_grad)

    mixer_all, low_all, gated_low, vec, residual, second_low = mix_front(
        place_all, weight_bits, weight_in, gathered, x, before, same
    )

    hidden_units = gate_proj.shape[1]
    bits_all = list(range(bits_of("mp") + bits_of("dp")))
    bits_all.append(bits_all.pop(bits_of("mp")))
    beside = swap(second_low, "mp", 0)
    across = swap(second_low, "mp", 1)
    *near_acts, og, ou, od = near_feed(
        [second_low, beside], group_grad[:2], gate_proj, up_proj, down_proj
    )
    near_grads = [og, ou, od]
    order.mark(near_grads[0])
    across = order(across)
    far = (
        place, [across, swap(across, "mp", 0)], group_grad[2:], gate_proj, up_proj, down_proj,
        near_grads,
    )
    wide = hidden_units // 3
    assert wide % LANES == 0
    far_acts, sums = (), []
    for n in range(3):
        far_acts, [pair] = far_feed(*far, far_acts, [(0, 1, 2)], wide, n)
        order.mark(pair[1])
        sums.append(Sum(order, *pair, (0, 1, 2)))
        if n == 0:
            sums[0].send()
    one, two, three = sums

    def back(acts, n):
        gate_low, up_low = order((acts[2 + n], acts[4 + n]))
        grad = dot(gate_low, gate_proj, NT) + dot(up_low, up_proj, NT)
        return order.mark(grad.astype(BF16))

    def both(kept, got):
        (total,) = halve(kept[None], order(got)[None], 1)
        return order.mark(total)[0]

    got = swap(back(far_acts, 1), "mp", 0)
    one.add()
    one.send()
    two.send()
    back_across = swap(both(back(far_acts, 0), got), "mp", 1)
    back_beside = swap(back(near_acts, 1), "mp", 0)
    one.add()
    one.send()
    back_near = back(near_acts, 0)
    hids = [near_acts[0], near_acts[1], far_acts[0], far_acts[1]]
    place_in = lax.axis_index("mp").reshape(1).astype(jnp.int32)
    parts = order.mark(onward(place_in, order(hids), down_proj))
    branch = lax.psum_scatter(parts, "mp", scatter_dimension=0, tiled=True)
    two.add()
    two.send()
    one.add()
    one.send()
    three.send()
    three.add()
    three.send()

    back_across, back_beside = order((back_across, back_beside))
    residual_grad, residual_low, closing_low, product_part, rim_out, totals = mix_back(
        place_all, weight_bits, back_near, back_beside, back_across, cotangent, residual,
        mixer_all, gathered, vec, same,
    )
    order.mark(rim_out)
    rim_back = shift(rim_out, "mp", -1)
    one.add()
    one.send()
    two.add()
    two.send()
    halves = mix_outer(
        place_all, bits_all, gated_low, order(residual_low), low_all, closing_low, totals
    )
    order.mark(halves[1])
    outer = Scatter(order, *halves, bits_all)
    outer.send()
    three.add()
    three.send()
    two.add()
    two.send()
    outer.add()
    outer.send()
    one.add()
    one.send()
    first_part, last_part, *halves = mix_grads(
        place_all, bits_all, product_part, order(rim_back), mixer_all, low_all
    )
    order.mark(halves[1])
    rest = Scatter(order, *halves, bits_all)
    rest.send()
    two.add()
    two.send()
    three.add()
    three.send()
    rest.add()
    rest.send()
    input_grad = input_back(
        order(first_part), closing_low, last_part, weight_in, residual_grad, x, vec,
    )
    order.mark(input_grad)
    input_grad = input_grad.reshape(1, rows, features)
    two.add()
    two.send()
    three.add()
    three.send()
    outer.add()
    outer.send()
    rest.add()
    rest.send()
    three.add()
    three.send()
    layer_out = order.mark((residual + order(branch).astype(F32)).astype(BF16))
    layer_out = layer_out.reshape(1, rows, features)
    one.add()
    done = unpack(place, one.pieces, (), one.bits, wide, 0, features, hidden_units)
    order.mark(done[0])
    outer.add()
    outer.send()
    rest.add()
    rest.send()
    outer.add()
    outer.send()
    rest.add()
    rest.send()
    outer.finish()
    two.add()
    done = unpack(place, two.pieces, done, two.bits, wide, 1, features, hidden_units)
    order.mark(done[0])
    rest.finish()
    grad_out = outer.total[:, :features]
    grad_second = outer.total[:, features]
    grad_conv = outer.total[:, features + 1 : features + 1 + KERNEL]
    ends = rest.total
    grad_in = jnp.concatenate(
        [ends[:, :features], outer.total[:, features + LANES :], ends[:, features:]], 1
    )
    grad_first = jnp.sum(grad_in * in_proj.astype(F32), axis=1) / first_gain.astype(F32)
    three.add()
    grad_gate, grad_up, grad_down = unpack(
        place, three.pieces, done, three.bits, wide, 2, features, hidden_units
    )
    return (
        layer_out,
        input_grad,
        grad_first,
        grad_in,
        grad_conv,
        grad_out,
        grad_second,
        grad_gate,
        grad_up,
        grad_down,
    )


def solution(mesh):
    in_specs = (
        P("dp", "mp", None),
        P("dp", "mp"),
        P(("dp", "mp")),
        P(("dp", "mp"), None),
        P(("dp", "mp"), None),
        P(("dp", "mp"), None),
        P(("dp", "mp")),
        P(None, "mp"),
        P(None, "mp"),
        P("mp", None),
        P("dp", "mp", None),
    )
    out_specs = (
        P("dp", "mp", None),
        P("dp", "mp", None),
        P(("dp", "mp")),
        P(("dp", "mp"), None),
        P(("dp", "mp"), None),
        P(("dp", "mp"), None),
        P(("dp", "mp")),
        P(None, "mp"),
        P(None, "mp"),
        P("mp", None),
    )
    return jax.shard_map(
        per_device, mesh=mesh, in_specs=in_specs, out_specs=out_specs, check_vma=False
    )
```

```python
import functools

import jax
import jax.numpy as jnp
from jax import lax
from jax.experimental import pallas as pl
from jax.experimental.pallas import tpu as pltpu
from jax.sharding import PartitionSpec as P

KERNEL = 3
LANES = 128
BF16 = jnp.bfloat16
F32 = jnp.float32
HALVINGS = 3
PARTS = 1 << HALVINGS
NN = (((1,), (0,)), ((), ()))
NT = (((1,), (1,)), ((), ()))
TN = (((0,), (0,)), ((), ()))
VMEM_LIMIT = 60 * 1024 * 1024
LONG = pl.CostEstimate(flops=10**11, transcendentals=0, bytes_accessed=0)

epsilon = 1e-05


def swap(block, axis, bit):
    size = lax.axis_size(axis)
    return lax.ppermute(block, axis, [(i, i ^ (1 << bit)) for i in range(size)])


def shift(block, axis, distance):
    devices = range(lax.axis_size(axis))
    route = [(i - distance, i) for i in devices if i - distance in devices]
    return lax.ppermute(block, axis, route)


def bit_of(axis, bit):
    return (lax.axis_index(axis) >> bit) & 1


def bits_of(axis):
    size = lax.axis_size(axis)
    assert size & (size - 1) == 0
    return size.bit_length() - 1


def after(values, *before):
    return lax.optimization_barrier((values, before))[0]


class Order:
    def __init__(self):
        self.last = ()

    def __call__(self, values):
        return after(values, self.last)

    def mark(self, out):
        self.last = out
        return out


def away(bits):
    top = len(bits) - 1
    return [sum(((q >> (top - n)) & 1) << bit for n, bit in enumerate(bits)) for q in range(PARTS)]


def dot(left, right, dims):
    return lax.dot_general(left, right, dims, preferred_element_type=F32)


def activate(gate_val, up_val, hidden_grad):
    sig = 1.0 / (1.0 + jnp.exp(-gate_val))
    silu = gate_val * sig
    return (
        (silu * up_val).astype(BF16),
        (hidden_grad * up_val * (sig * (1.0 + gate_val * (1.0 - sig)))).astype(BF16),
        (hidden_grad * silu).astype(BF16),
    )


def feed(x_ref, go_ref, gate_ref, up_ref, down_ref, acts, outs):
    for n in range(2):
        step = x_ref.shape[0] // 2
        part = slice(n * step, (n + 1) * step)
        gate_val = dot(x_ref[part], gate_ref[...], NN)
        up_val = dot(x_ref[part], up_ref[...], NN)
        hidden_grad = dot(go_ref[part], down_ref[...], NT)
        for m, value in enumerate(activate(gate_val, up_val, hidden_grad)):
            acts[m][part] = value
            outs[2 * m + n][...] = value


def join(first, xa_ref, xb_ref, ga_ref, gb_ref, x_ref, go_ref):
    rows = xa_ref.shape[0]

    @pl.when(first)
    def _():
        x_ref[:rows] = xa_ref[...]
        x_ref[rows:] = xb_ref[...]
        go_ref[:rows] = ga_ref[...]
        go_ref[rows:] = gb_ref[...]


def near_kernel(xa_ref, xb_ref, ga_ref, gb_ref, gate_ref, up_ref, down_ref,
                *refs):
    outs = refs[:6]
    og_ref, ou_ref, od_ref, x_ref, go_ref, hid_ref, gl_ref, ul_ref = refs[6:]
    join(pl.program_id(0) == 0, xa_ref, xb_ref, ga_ref, gb_ref, x_ref, go_ref)
    feed(x_ref, go_ref, gate_ref, up_ref, down_ref, (hid_ref, gl_ref, ul_ref), outs)
    og_ref[...] = dot(x_ref[...], gl_ref[...], TN).astype(BF16)
    ou_ref[...] = dot(x_ref[...], ul_ref[...], TN).astype(BF16)
    od_ref[...] = dot(hid_ref[...], go_ref[...], TN).astype(BF16)


def near_feed(xs, gos, gate, up, down):
    rows, features = xs[0].shape
    hidden = gate.shape[1]
    wide = 256
    tokens = 2 * rows
    whole = pl.BlockSpec((rows, features), lambda i: (0, 0), pipeline_mode=pl.Buffered(1))
    col = pl.BlockSpec((features, wide), lambda i: (0, i))
    row = pl.BlockSpec((wide, features), lambda i: (i, 0))
    act = pl.BlockSpec((rows, wide), lambda i: (0, i))
    return pl.pallas_call(
        near_kernel,
        grid=(pl.cdiv(hidden, wide),),
        in_specs=[whole] * 4 + [col, col, row],
        out_specs=[act] * 6 + [col, col, row],
        out_shape=[jax.ShapeDtypeStruct((rows, hidden), BF16)] * 6
        + [jax.ShapeDtypeStruct((features, hidden), BF16)] * 2
        + [jax.ShapeDtypeStruct((hidden, features), BF16)],
        scratch_shapes=[pltpu.VMEM((tokens, features), BF16)] * 2
        + [pltpu.VMEM((tokens, wide), BF16)] * 3,
        compiler_params=pltpu.CompilerParams(vmem_limit_bytes=VMEM_LIMIT),
        cost_estimate=LONG,
        name="near_feed",
    )(*xs, *gos, gate, up, down)


def far_kernel(orders, place_ref, xa_ref, xb_ref, ga_ref, gb_ref, gate_ref, up_ref, down_ref,
               ng_ref, nu_ref, nd_ref, *refs):
    blocks = len(orders)
    x_ref, go_ref, tg_ref, tu_ref, td_ref, hid_ref, gl_ref, ul_ref = refs[-8:]
    packs = refs[-8 - 2 * blocks : -8]
    outs = refs[-14 - 2 * blocks : -8 - 2 * blocks]
    now = pl.program_id(0)
    join(now == 0, xa_ref, xb_ref, ga_ref, gb_ref, x_ref, go_ref)
    feed(x_ref, go_ref, gate_ref, up_ref, down_ref, (hid_ref, gl_ref, ul_ref), outs)
    tg_ref[...] = ng_ref[...].astype(F32) + dot(x_ref[...], gl_ref[...], TN)
    tu_ref[...] = nu_ref[...].astype(F32) + dot(x_ref[...], ul_ref[...], TN)
    td_ref[...] = nd_ref[...].astype(F32) + dot(hid_ref[...], go_ref[...], TN)
    features, wide = tg_ref.shape
    tall, low = features // PARTS, wide // PARTS
    for n, bits in enumerate(orders):

        @pl.when(now == n)
        def _(n=n, bits=bits):
            for q, far in enumerate(away(bits or (0, 1, 2))):
                part = place_ref[0] ^ far if bits else far
                half = PARTS // 2
                out = packs[2 * n + q // half].at[q % half]
                rows = pl.ds(part * tall, tall)
                at = 0
                for grad_ref in (tg_ref, tu_ref):
                    for c in range(0, wide, LANES):
                        out[at : at + tall] = grad_ref[rows, c : c + LANES].astype(BF16)
                        at += tall
                rows = pl.ds(part * low, low)
                for c in range(0, features, LANES):
                    out[at : at + low] = td_ref[rows, c : c + LANES].astype(BF16)
                    at += low


def far_feed(place, xs, gos, gate, up, down, near_grads, before, orders, wide, index):
    rows, features = xs[0].shape
    tokens = 2 * rows
    hidden = gate.shape[1]
    blocks = len(orders)
    whole = pl.BlockSpec((rows, features), lambda i, _: (0, 0), pipeline_mode=pl.Buffered(1))
    col = pl.BlockSpec((features, wide), lambda i, _: (0, index + i))
    row = pl.BlockSpec((wide, features), lambda i, _: (index + i, 0))
    act = pl.BlockSpec((rows, wide), lambda i, _: (0, index + i))
    packed = 3 * features * wide // PARTS // LANES
    half = pl.BlockSpec((PARTS // 2, packed, LANES), lambda i, _: (0, 0, 0), pipeline_mode=pl.Buffered(1))
    first = 1 + 4 + 3 + 3
    results = pl.pallas_call(
        functools.partial(far_kernel, orders),
        grid_spec=pltpu.PrefetchScalarGridSpec(
            num_scalar_prefetch=1,
            grid=(blocks,),
            in_specs=[whole] * 4
            + [col, col, row] * 2
            + [pl.BlockSpec(memory_space=pl.ANY)] * len(before),
            out_specs=[act] * 6 + [half] * (2 * blocks),
            scratch_shapes=[pltpu.VMEM((tokens, features), BF16)] * 2
            + [pltpu.VMEM((features, wide), F32)] * 2
            + [pltpu.VMEM((wide, features), F32)]
            + [pltpu.VMEM((tokens, wide), BF16)] * 3,
        ),
        out_shape=[jax.ShapeDtypeStruct((rows, hidden), BF16)] * 6
        + [jax.ShapeDtypeStruct((PARTS // 2, packed, LANES), BF16)] * (2 * blocks),
        input_output_aliases={first + n: n for n in range(len(before))},
        compiler_params=pltpu.CompilerParams(vmem_limit_bytes=VMEM_LIMIT),
        cost_estimate=LONG,
        name="far_feed",
    )(place, *xs, *gos, gate, up, down, *near_grads, *before)
    return results[:6], list(zip(results[6::2], results[7::2]))


def unpack_kernel(bits, pieces, place_ref, *refs):
    og_ref, ou_ref, od_ref = refs[-3:]
    features, wide = og_ref.shape
    tall, low = features // PARTS, wide // PARTS
    sources = [ref.at[n] for ref in refs[:pieces] for n in range(ref.shape[0])]
    for source, far in zip(sources, away(bits or (0, 1, 2))):
        part = place_ref[0] ^ far if bits else far
        rows = pl.ds(part * tall, tall)
        at = 0
        for out in (og_ref, ou_ref):
            for c in range(0, wide, LANES):
                out[rows, c : c + LANES] = source[at : at + tall].astype(F32)
                at += tall
        rows = pl.ds(part * low, low)
        for c in range(0, features, LANES):
            od_ref[rows, c : c + LANES] = source[at : at + low].astype(F32)
            at += low


def unpack(place, pieces, before, bits, wide, index, features, hidden):
    packed = pieces[0].shape[1]
    ins = [
        pl.BlockSpec((piece.shape[0], packed, LANES), lambda i, _: (0, 0, 0)) for piece in pieces
    ]
    col = pl.BlockSpec((features, wide), lambda i, _: (0, index))
    row = pl.BlockSpec((wide, features), lambda i, _: (index, 0))
    keep = [pl.BlockSpec(memory_space=pl.ANY)] * len(before)
    return pl.pallas_call(
        functools.partial(unpack_kernel, bits, len(pieces)),
        grid_spec=pltpu.PrefetchScalarGridSpec(
            num_scalar_prefetch=1,
            grid=(1,),
            in_specs=ins + keep,
            out_specs=[col, col, row],
        ),
        out_shape=[jax.ShapeDtypeStruct((features, hidden), F32)] * 2
        + [jax.ShapeDtypeStruct((hidden, features), F32)],
        input_output_aliases={1 + len(ins) + n: n for n in range(len(before))},
        compiler_params=pltpu.CompilerParams(vmem_limit_bytes=VMEM_LIMIT),
        cost_estimate=LONG,
        name="unpack",
    )(place, *pieces, *before)


def add_low(one, two):
    return (one.astype(F32) + two.astype(F32)).astype(BF16)


def whole(array):
    return pl.BlockSpec(array.shape, lambda i: (0,) * array.ndim)


def halve_kernel(kept_ref, got_ref, *outs):
    half = outs[-1].shape[0]
    for n, out in enumerate(outs):
        part = slice(n * half, (n + 1) * half)
        out[...] = (kept_ref[part].astype(F32) + got_ref[part].astype(F32)).astype(out.dtype)


def halve(kept, got, halves=2, dtype=BF16):
    count, tall, wide = kept.shape
    shapes = [jax.ShapeDtypeStruct((count // halves, tall, wide), dtype)] * halves
    return pl.pallas_call(
        halve_kernel,
        grid=(1,),
        in_specs=[whole(kept), whole(got)],
        out_specs=[whole(s) for s in shapes],
        out_shape=shapes,
        compiler_params=pltpu.CompilerParams(vmem_limit_bytes=VMEM_LIMIT),
        cost_estimate=LONG,
        name="halve",
    )(kept, got)


def lay_kernel(*refs):
    at = 0
    for ref in refs[:-1]:
        refs[-1][at : at + ref.shape[0]] = ref[...]
        at += ref.shape[0]


def lay(pieces):
    _, tall, wide = pieces[0].shape
    shape = jax.ShapeDtypeStruct((sum(p.shape[0] for p in pieces), tall, wide), pieces[0].dtype)
    return pl.pallas_call(
        lay_kernel,
        grid=(1,),
        in_specs=[whole(p) for p in pieces],
        out_specs=whole(shape),
        out_shape=shape,
        compiler_params=pltpu.CompilerParams(vmem_limit_bytes=VMEM_LIMIT),
        cost_estimate=LONG,
        name="lay",
    )(*pieces)


def pack_rows(place, bits, grad_ref, kept_ref, sent_ref, lane):
    count = len(bits)
    half, tall, _ = kept_ref.shape
    wide = grad_ref.shape[1]

    def move(q, out_ref, slot):
        far = 0
        for n, bit in enumerate(bits):
            far = far | (((q >> (count - 1 - n)) & 1) << bit)
        rows = pl.ds(pl.multiple_of((place ^ far) * tall, tall), tall)
        out_ref[slot, :, lane : lane + wide] = grad_ref[rows].astype(BF16)

    @pl.loop(0, half)
    def _(q):
        move(q, kept_ref, q)
        move(q + half, sent_ref, q)


STRIP = 64
RIM = 8


def fold(values):
    return jnp.sum(values.reshape(values.shape[0] // 8, 8, values.shape[1]), axis=0)


def assemble(place, bits, sources, width, target_ref, lane, sems):
    half, tall, _ = sources[0][0].shape
    count = len(bits)

    def copy(q, n):
        ref, start = sources[n]
        far = 0
        for m, bit in enumerate(bits):
            far = far | ((((q + n * half) >> m) & 1) << bit)
        rows = pl.ds(pl.multiple_of((place ^ far) * tall, tall), tall)
        return pltpu.make_async_copy(
            ref.at[q, :, start : start + width],
            target_ref.at[rows, lane : lane + width],
            sems.at[n * half + q],
        )

    @pl.loop(0, half)
    def _(q):
        for n in range(2):
            copy(q, n).start()

    def wait():
        @pl.loop(0, half)
        def _(q):
            for n in range(2):
                copy(q, n).wait()

    return wait


def mix_front_kernel(bits, place_ref, in_any, c0, c1, x_ref, before_ref, same_ref,
                     mix_any, low_any, gated_any, vec_ref, res_ref, second_ref,
                     w_ref, wo_ref, mix_ref, low_ref, gated_ref, ext_ref, sems, in_sem, out_sem):
    place = place_ref[0]
    rows, features = x_ref.shape
    last = features + LANES
    wide = features
    loads = [
        pltpu.make_async_copy(
            in_any.at[:, n * wide : (n + 1) * wide], w_ref.at[:, n * wide : (n + 1) * wide], in_sem.at[n]
        )
        for n in range(3)
    ]
    wait_out = assemble(place, bits, [(c0, 0), (c1, 0)], features + LANES, wo_ref, 0, sems)
    for load in loads:
        load.start()
    wait_out()
    vec_ref[...] = wo_ref[:, features:].astype(F32).T[:8]
    gain_one, gain_two = vec_ref[0:1], vec_ref[1:2]
    taps = [vec_ref[2 + k : 3 + k] for k in range(KERNEL)]

    def normed(values, gain):
        inverse = lax.rsqrt(jnp.mean(values * values, axis=-1, keepdims=True) + epsilon)
        return (values * inverse * gain).astype(BF16)

    low_ref[:RIM] = normed(before_ref[...].astype(F32), gain_one)

    @pl.loop(0, rows // STRIP)
    def _(i):
        at = pl.ds(pl.multiple_of(i * STRIP, STRIP), STRIP)
        inner = pl.ds(pl.multiple_of(i * STRIP + RIM, RIM), STRIP)
        low_ref[inner] = normed(x_ref[at].astype(F32), gain_one)

    stores = [pltpu.make_async_copy(low_ref, low_any, out_sem.at[0])]
    stores[0].start()
    for n, load in enumerate(loads):
        load.wait()
        part = slice(n * wide, (n + 1) * wide)
        mix_ref[:, part] = dot(low_ref[...], w_ref[:, part], NN)
        stores.append(
            pltpu.make_async_copy(mix_ref.at[:, part], mix_any.at[:, part], out_sem.at[1 + n])
        )
        stores[-1].start()
    ext_ref[:RIM] = mix_ref[:RIM, :features] * mix_ref[:RIM, 2 * features :]

    @pl.loop(0, rows // STRIP)
    def _(i):
        at = pl.ds(pl.multiple_of(i * STRIP + RIM, RIM), STRIP)
        ext_ref[at] = mix_ref[at, :features] * mix_ref[at, 2 * features :]

    @pl.loop(0, rows // STRIP)
    def _(i):
        at = pl.ds(pl.multiple_of(i * STRIP, STRIP), STRIP)
        inner = pl.ds(pl.multiple_of(i * STRIP + RIM, RIM), STRIP)
        window = ext_ref[pl.ds(pl.multiple_of(i * STRIP, STRIP), STRIP + RIM)]
        skip = RIM - (KERNEL - 1)
        conv = 0.0
        for k in range(KERNEL):
            same = same_ref[at, k : k + 1] > 0.5
            conv += jnp.where(same, window[skip + k : skip + k + STRIP], 0.0) * taps[k]
        gated_ref[at] = (mix_ref[inner, features : 2 * features] * conv).astype(BF16)

    stores.append(pltpu.make_async_copy(gated_ref, gated_any, out_sem.at[4]))
    stores[-1].start()
    res_ref[...] = dot(gated_ref[...], wo_ref[:, :features], NN)

    @pl.loop(0, rows // STRIP)
    def _(i):
        at = pl.ds(pl.multiple_of(i * STRIP, STRIP), STRIP)
        residual = x_ref[at].astype(F32) + res_ref[at]
        res_ref[at] = residual
        second_ref[at] = normed(residual, gain_two)

    for store in stores:
        store.wait()


def mix_front(place, bits, weight_in, gathered, x, before, same):
    rows, features = x.shape
    anywhere = pl.BlockSpec(memory_space=pl.ANY)
    outs = [
        jax.ShapeDtypeStruct((rows + RIM, 3 * features), F32),
        jax.ShapeDtypeStruct((rows + RIM, features), BF16),
        jax.ShapeDtypeStruct((rows, features), BF16),
        jax.ShapeDtypeStruct((8, features), F32),
        jax.ShapeDtypeStruct((rows, features), F32),
        jax.ShapeDtypeStruct((rows, features), BF16),
    ]
    return pl.pallas_call(
        functools.partial(mix_front_kernel, bits),
        grid_spec=pltpu.PrefetchScalarGridSpec(
            num_scalar_prefetch=1,
            grid=(1,),
            in_specs=[anywhere] * 3 + [once(x), once(before), once(same)],
            out_specs=[anywhere] * 3 + [once(s) for s in outs[3:]],
            scratch_shapes=[
                pltpu.VMEM((features, 3 * features), BF16),
                pltpu.VMEM((features, features + LANES), BF16),
                pltpu.VMEM((rows + RIM, 3 * features), F32),
                pltpu.VMEM((rows + RIM, features), BF16),
                pltpu.VMEM((rows, features), BF16),
                pltpu.VMEM((rows + RIM, features), F32),
                pltpu.SemaphoreType.DMA((1 << len(bits),)),
                pltpu.SemaphoreType.DMA((3,)),
                pltpu.SemaphoreType.DMA((5,)),
            ],
        ),
        out_shape=outs,
        compiler_params=pltpu.CompilerParams(vmem_limit_bytes=VMEM_LIMIT),
        cost_estimate=LONG,
        name="mix_front",
    )(place, weight_in, *gathered, x, before, same)


def onward_kernel(place_ref, *refs):
    *hids, down_ref, out_ref = refs
    for n, hid_ref in enumerate(hids):

        @pl.when(pl.program_id(0) == n)
        def _(hid_ref=hid_ref):
            out_ref[...] = dot(hid_ref[...], down_ref[...], NN).astype(BF16)


def onward(place, hids, down):
    rows, hidden = hids[0].shape
    features = down.shape[1]
    return pl.pallas_call(
        onward_kernel,
        grid_spec=pltpu.PrefetchScalarGridSpec(
            num_scalar_prefetch=1,
            grid=(len(hids),),
            in_specs=[once(a) for a in (*hids, down)],
            out_specs=pl.BlockSpec((rows, features), lambda i, place: (place[0] ^ i, 0)),
        ),
        out_shape=jax.ShapeDtypeStruct((len(hids) * rows, features), BF16),
        compiler_params=pltpu.CompilerParams(vmem_limit_bytes=VMEM_LIMIT),
        cost_estimate=LONG,
        name="onward",
    )(place, *hids, down)


def mix_back_kernel(bits, place_ref, near_ref, beside_ref, across_ref, cot_ref, res_ref, mix_ref,
                    c0, c1, vec_ref, same_ref,
                    rg_ref, rlow_ref, cl_ref, pg_ref, rim_ref, sums_ref,
                    ext_ref, gg_ref, d0_ref, d1_ref, d2_ref, w_ref, sems):
    rows, features = res_ref.shape
    wait = assemble(place_ref[0], bits, [(c0, 0), (c1, 0)], features, w_ref, 0, sems)
    sums_ref[...] = jnp.zeros_like(sums_ref)
    gain = vec_ref[1:2]
    taps = [vec_ref[2 + k : 3 + k] for k in range(KERNEL)]

    @pl.loop(0, rows // STRIP)
    def _(i):
        at = pl.ds(pl.multiple_of(i * STRIP, STRIP), STRIP)
        second = near_ref[at].astype(F32) + beside_ref[at].astype(F32) + across_ref[at].astype(F32)
        residual = res_ref[at]
        inverse = lax.rsqrt(jnp.mean(residual * residual, axis=-1, keepdims=True) + epsilon)
        unit = residual * inverse
        weighted = second * gain
        mean = jnp.mean(weighted * unit, axis=-1, keepdims=True)
        grad = cot_ref[at].astype(F32) + inverse * (weighted - unit * mean)
        rg_ref[at] = grad
        rlow_ref[at] = grad.astype(BF16)
        sums_ref[0] += fold(second * unit)

    wait()
    gg_ref[...] = dot(rlow_ref[...], w_ref[...], NT)
    ext_ref[:RIM] = mix_ref[:RIM, :features] * mix_ref[:RIM, 2 * features :]

    @pl.loop(0, rows // STRIP)
    def _(i):
        at = pl.ds(pl.multiple_of(i * STRIP + RIM, RIM), STRIP)
        ext_ref[at] = mix_ref[at, :features] * mix_ref[at, 2 * features :]

    zeros = jnp.zeros((RIM, features), F32)
    for d_ref in (d0_ref, d1_ref, d2_ref):
        d_ref[:RIM] = zeros
        d_ref[rows + RIM :] = zeros

    @pl.loop(0, rows // STRIP)
    def _(i):
        at = pl.ds(pl.multiple_of(i * STRIP, STRIP), STRIP)
        inner = pl.ds(pl.multiple_of(i * STRIP + RIM, RIM), STRIP)
        window = ext_ref[pl.ds(pl.multiple_of(i * STRIP, STRIP), STRIP + RIM)]
        skip = RIM - (KERNEL - 1)
        same = [same_ref[at, k : k + 1] > 0.5 for k in range(KERNEL)]
        past = [
            jnp.where(same[k], window[skip + k : skip + k + STRIP], 0.0) for k in range(KERNEL)
        ]
        conv = past[0] * taps[0] + past[1] * taps[1] + past[2] * taps[2]
        gated_grad = gg_ref[at]
        cl_ref[at] = (gated_grad * conv).astype(BF16)
        conv_grad = gated_grad * mix_ref[inner, features : 2 * features]
        for k, d_ref in enumerate((d0_ref, d1_ref, d2_ref)):
            sums_ref[1 + k] += fold(conv_grad * past[k])
            d_ref[inner] = jnp.where(same[k], conv_grad * taps[k], 0.0)

    rim_ref[...] = d0_ref[2 : 2 + RIM] + d1_ref[1 : 1 + RIM]

    @pl.loop(0, rows // STRIP)
    def _(i):
        at = pl.ds(pl.multiple_of(i * STRIP, STRIP), STRIP)
        window = pl.ds(pl.multiple_of(i * STRIP + RIM, RIM), STRIP + RIM)
        inner = pl.ds(pl.multiple_of(i * STRIP + RIM, RIM), STRIP)
        pg_ref[at] = (
            d2_ref[inner] + d1_ref[window][1 : 1 + STRIP] + d0_ref[window][2 : 2 + STRIP]
        )


def mix_outer_kernel(bits, place_ref, gated_ref, rlow_ref, low_ref, cl_ref, sums_ref,
                     out_kept, out_sent, acc_ref):
    place = place_ref[0]
    features = acc_ref.shape[0]
    acc_ref[...] = dot(gated_ref[...], rlow_ref[...], TN)
    pack_rows(place, bits, acc_ref, out_kept, out_sent, 0)
    totals = jnp.sum(sums_ref[...], axis=1)
    totals = jnp.concatenate([totals, jnp.zeros_like(totals)], 0)[:8].astype(BF16)
    units = lax.broadcasted_iota(jnp.int32, (8, LANES), 0) == lax.broadcasted_iota(
        jnp.int32, (8, LANES), 1
    )
    acc_ref[:, :LANES] = dot(totals, jnp.where(units, 1.0, 0.0).astype(BF16), TN)
    pack_rows(place, bits, acc_ref.at[:, :LANES], out_kept, out_sent, features)
    acc_ref[...] = dot(low_ref[RIM:], cl_ref[...], TN)
    pack_rows(place, bits, acc_ref, out_kept, out_sent, features + LANES)


def once(array):
    return pl.BlockSpec(array.shape, lambda *_: (0,) * array.ndim, pipeline_mode=pl.Buffered(1))


def mix_back(place, bits, near, beside, across, cot, res, mix, gathered, vec, same):
    rows, features = res.shape
    shapes = [
        jax.ShapeDtypeStruct((rows, features), F32),
        jax.ShapeDtypeStruct((rows, features), BF16),
        jax.ShapeDtypeStruct((rows, features), BF16),
        jax.ShapeDtypeStruct((rows, features), F32),
        jax.ShapeDtypeStruct((RIM, features), F32),
        jax.ShapeDtypeStruct((1 + KERNEL, 8, features), F32),
    ]
    ins = [near, beside, across, cot, res, mix]
    anywhere = pl.BlockSpec(memory_space=pl.ANY)
    return pl.pallas_call(
        functools.partial(mix_back_kernel, bits),
        grid_spec=pltpu.PrefetchScalarGridSpec(
            num_scalar_prefetch=1,
            grid=(1,),
            in_specs=[once(a) for a in ins] + [anywhere] * 2 + [once(vec), once(same)],
            out_specs=[once(s) for s in shapes],
            scratch_shapes=[
                pltpu.VMEM((rows + RIM, features), F32),
                pltpu.VMEM((rows, features), F32),
                *[pltpu.VMEM((rows + 2 * RIM, features), F32)] * 3,
                pltpu.VMEM((features, features), BF16),
                pltpu.SemaphoreType.DMA((1 << len(bits),)),
            ],
        ),
        out_shape=shapes,
        compiler_params=pltpu.CompilerParams(vmem_limit_bytes=VMEM_LIMIT),
        cost_estimate=LONG,
        name="mix_back",
    )(place, *ins, *gathered, vec, same)


def mix_outer(place, bits, gated, rlow, low, cl, sums):
    features = gated.shape[1]
    parts = 1 << len(bits)
    ins = [gated, rlow, low, cl, sums]
    shapes = [
        jax.ShapeDtypeStruct((parts // 2, features // parts, 2 * features + LANES), BF16)
    ] * 2
    return pl.pallas_call(
        functools.partial(mix_outer_kernel, bits),
        grid_spec=pltpu.PrefetchScalarGridSpec(
            num_scalar_prefetch=1,
            grid=(1,),
            in_specs=[once(a) for a in ins],
            out_specs=[once(s) for s in shapes],
            scratch_shapes=[pltpu.VMEM((features, features), F32)],
        ),
        out_shape=shapes,
        compiler_params=pltpu.CompilerParams(vmem_limit_bytes=VMEM_LIMIT),
        cost_estimate=LONG,
        name="mix_outer",
    )(place, *ins)


def mix_grads_kernel(bits, place_ref, pg_ref, rim_ref, mix_ref, low_ref,
                     first_ref, last_ref, kept_ref, sent_ref, acc_ref):
    place = place_ref[0]
    rows, features = pg_ref.shape

    @pl.loop(0, rows // STRIP)
    def _(i):
        at = pl.ds(pl.multiple_of(i * STRIP, STRIP), STRIP)
        inner = pl.ds(pl.multiple_of(i * STRIP + RIM, RIM), STRIP)
        grad = pg_ref[at]
        first_ref[at] = (grad * mix_ref[inner, 2 * features :]).astype(BF16)
        last_ref[at] = (grad * mix_ref[inner, :features]).astype(BF16)

    grad = pg_ref[rows - RIM :] + rim_ref[...]
    first_ref[rows - RIM :] = (grad * mix_ref[rows:, 2 * features :]).astype(BF16)
    last_ref[rows - RIM :] = (grad * mix_ref[rows:, :features]).astype(BF16)
    for n, grad_ref in enumerate((first_ref, last_ref)):
        acc_ref[...] = dot(low_ref[RIM:], grad_ref[...], TN)
        pack_rows(place, bits, acc_ref, kept_ref, sent_ref, n * features)


def mix_grads(place, bits, pg, rim, mix, low):
    rows, features = pg.shape
    parts = 1 << len(bits)
    tall = features // parts

    def whole(array):
        return pl.BlockSpec(
            array.shape, lambda i, _: (0,) * array.ndim, pipeline_mode=pl.Buffered(1)
        )

    shapes = [jax.ShapeDtypeStruct((rows, features), BF16)] * 2
    shapes += [jax.ShapeDtypeStruct((parts // 2, tall, 2 * features), BF16)] * 2
    return pl.pallas_call(
        functools.partial(mix_grads_kernel, bits),
        grid_spec=pltpu.PrefetchScalarGridSpec(
            num_scalar_prefetch=1,
            grid=(1,),
            in_specs=[whole(a) for a in (pg, rim, mix, low)],
            out_specs=[whole(s) for s in shapes],
            scratch_shapes=[pltpu.VMEM((features, features), F32)],
        ),
        out_shape=shapes,
        compiler_params=pltpu.CompilerParams(vmem_limit_bytes=VMEM_LIMIT),
        cost_estimate=LONG,
        name="mix_grads",
    )(place, pg, rim, mix, low)


def input_back_kernel(first_ref, mid_ref, last_ref, w_ref, rg_ref, x_ref, vec_ref, out_ref, fg_ref):
    rows, features = rg_ref.shape
    fg_ref[...] = dot(first_ref[...], w_ref[:, :features], NT)
    fg_ref[...] += dot(mid_ref[...], w_ref[:, features : 2 * features], NT)
    fg_ref[...] += dot(last_ref[...], w_ref[:, 2 * features :], NT)

    @pl.loop(0, rows // STRIP)
    def _(i):
        at = pl.ds(pl.multiple_of(i * STRIP, STRIP), STRIP)
        values = x_ref[at].astype(F32)
        inverse = lax.rsqrt(jnp.mean(values * values, axis=-1, keepdims=True) + epsilon)
        unit = values * inverse
        weighted = fg_ref[at] * vec_ref[0:1]
        mean = jnp.mean(weighted * unit, axis=-1, keepdims=True)
        out_ref[at] = rg_ref[at] + inverse * (weighted - unit * mean)


def input_back(first, mid, last, weight_in, rg, x, vec):
    rows, features = rg.shape
    ins = [first, mid, last, weight_in, rg, x, vec]
    return pl.pallas_call(
        input_back_kernel,
        grid=(1,),
        in_specs=[once(a) for a in ins],
        out_specs=once(rg),
        out_shape=jax.ShapeDtypeStruct((rows, features), F32),
        scratch_shapes=[pltpu.VMEM((rows, features), F32)],
        compiler_params=pltpu.CompilerParams(vmem_limit_bytes=VMEM_LIMIT),
        cost_estimate=LONG,
        name="input_back",
    )(*ins)


def gather_mp(own):
    size = lax.axis_size("mp")
    blocks = [own] + [None] * (size - 1)
    for bit in reversed(range(bits_of("mp"))):
        for r in [r for r in range(size) if blocks[r] is not None]:
            blocks[r ^ (1 << bit)] = swap(blocks[r], "mp", bit)
    return blocks


class Sum:
    def __init__(self, order, kept, sent, bits):
        self.order, self.kept, self.sent, self.bits, self.step = order, kept, sent, bits, 0

    def send(self):
        steps = len(self.bits)
        bit = self.bits[self.step] if self.step < steps else self.bits[2 * steps - 1 - self.step]
        self.got = swap(self.sent, "dp", bit)

    def add(self):
        self.step += 1
        steps = len(self.bits)
        got = self.order(self.got)
        if self.step < steps:
            self.kept, self.sent = halve(self.kept, got)
        elif self.step == steps:
            (own,) = halve(self.kept, got, 1)
            for bit in range(HALVINGS, bits_of("dp")):
                (own,) = halve(own, swap(own, "dp", bit), 1)
            self.pieces = [own]
            self.sent = own
        else:
            self.pieces.append(got)
            if self.step == 2 * steps:
                return
            self.sent = lay(self.pieces)
        self.order.mark(self.sent)


class Scatter:
    def __init__(self, order, kept, sent, bits):
        self.order, self.kept, self.sent, self.bits, self.step = order, kept, sent, bits, 0

    def send(self):
        inner = bits_of("mp")
        bit = self.bits[self.step]
        axis, bit = ("mp", bit) if bit < inner else ("dp", bit - inner)
        self.got = swap(self.sent, axis, bit)

    def add(self):
        self.step += 1
        got = self.order(self.got)
        if self.step < len(self.bits):
            self.kept, self.sent = halve(self.kept, got)
            self.order.mark(self.sent)
        else:
            (total,) = halve(self.kept, got, 1, F32)
            self.total = self.order.mark(total)[0]

    def finish(self):
        while self.step < len(self.bits):
            self.add()
            if self.step < len(self.bits):
                self.send()


def per_device(
    block_in,
    segment_ids,
    first_gain,
    in_proj,
    conv_kernel,
    out_proj,
    second_gain,
    gate_proj,
    up_proj,
    down_proj,
    out_grad,
):
    rows = block_in.shape[1]
    features = block_in.shape[2]
    x = block_in.reshape(rows, features)
    own_ids = segment_ids.reshape(rows)
    cotangent = out_grad.reshape(rows, features)
    inner = lax.axis_size("mp")
    place = (lax.axis_index("dp") % PARTS).reshape(1).astype(jnp.int32)
    place_all = (lax.axis_index("dp") * inner + lax.axis_index("mp")).reshape(1).astype(jnp.int32)
    order = Order()

    def swap_all(block, bit):
        outer = bit - bits_of("mp")
        return swap(block, "mp", bit) if outer < 0 else swap(block, "dp", outer)

    before = shift(x[rows - RIM :], "mp", 1)
    ids_before = shift(own_ids[rows - RIM :].astype(F32), "mp", 1).astype(jnp.int32)
    ids_before = jnp.where(lax.axis_index("mp") == 0, -1, ids_before)
    ids = jnp.concatenate([ids_before, own_ids], 0)
    skip = RIM - (KERNEL - 1)
    same = [(ids[skip + k : skip + k + rows] == own_ids)[:, None] for k in range(KERNEL)]
    same = jnp.pad(jnp.concatenate(same, 1).astype(F32), ((0, 0), (0, LANES - KERNEL)))

    weight_in = lax.all_gather(in_proj, ("dp", "mp"), axis=0, tiled=True)
    small = jnp.concatenate(
        [first_gain[:, None], second_gain[:, None], conv_kernel], 1
    )
    small = jnp.pad(small, ((0, 0), (0, LANES - small.shape[1])))
    weight_bits = list(reversed(range(bits_of("mp") + bits_of("dp"))))
    gathered = [jnp.concatenate([out_proj, small], 1)[None]]
    for bit in weight_bits:
        held = jnp.concatenate(gathered, 0)
        gathered = [held, swap_all(held, bit)]
    group_grad = gather_mp(cotangent)
    weight_in = after(weight_in, gathered, before, group_grad)

    mixer_all, low_all, gated_low, vec, residual, second_low = mix_front(
        place_all, weight_bits, weight_in, gathered, x, before, same
    )

    hidden_units = gate_proj.shape[1]
    bits_all = list(range(bits_of("mp") + bits_of("dp")))
    bits_all.append(bits_all.pop(bits_of("mp")))
    beside = swap(second_low, "mp", 0)
    across = swap(second_low, "mp", 1)
    *near_acts, og, ou, od = near_feed(
        [second_low, beside], group_grad[:2], gate_proj, up_proj, down_proj
    )
    near_grads = [og, ou, od]
    order.mark(near_grads[0])
    across = order(across)
    far = (
        place, [across, swap(across, "mp", 0)], group_grad[2:], gate_proj, up_proj, down_proj,
        near_grads,
    )
    wide = hidden_units // 3
    assert wide % LANES == 0
    far_acts, sums = (), []
    for n in range(3):
        far_acts, [pair] = far_feed(*far, far_acts, [(0, 1, 2)], wide, n)
        order.mark(pair[1])
        sums.append(Sum(order, *pair, (0, 1, 2)))
        if n == 0:
            sums[0].send()
    one, two, three = sums

    def back(acts, n):
        gate_low, up_low = order((acts[2 + n], acts[4 + n]))
        grad = dot(gate_low, gate_proj, NT) + dot(up_low, up_proj, NT)
        return order.mark(grad.astype(BF16))

    def both(kept, got):
        (total,) = halve(kept[None], order(got)[None], 1)
        return order.mark(total)[0]

    got = swap(back(far_acts, 1), "mp", 0)
    one.add()
    one.send()
    two.send()
    back_across = swap(both(back(far_acts, 0), got), "mp", 1)
    back_beside = swap(back(near_acts, 1), "mp", 0)
    one.add()
    one.send()
    back_near = back(near_acts, 0)
    hids = [near_acts[0], near_acts[1], far_acts[0], far_acts[1]]
    place_in = lax.axis_index("mp").reshape(1).astype(jnp.int32)
    parts = order.mark(onward(place_in, order(hids), down_proj))
    branch = lax.psum_scatter(parts, "mp", scatter_dimension=0, tiled=True)
    two.add()
    two.send()
    one.add()
    one.send()
    three.send()
    three.add()
    three.send()

    back_across, back_beside = order((back_across, back_beside))
    residual_grad, residual_low, closing_low, product_part, rim_out, totals = mix_back(
        place_all, weight_bits, back_near, back_beside, back_across, cotangent, residual,
        mixer_all, gathered, vec, same,
    )
    order.mark(rim_out)
    rim_back = shift(rim_out, "mp", -1)
    two.add()
    two.send()
    one.add()
    one.send()
    halves = mix_outer(
        place_all, bits_all, gated_low, order(residual_low), low_all, closing_low, totals
    )
    order.mark(halves[1])
    outer = Scatter(order, *halves, bits_all)
    outer.send()
    three.add()
    three.send()
    outer.add()
    outer.send()
    two.add()
    two.send()
    one.add()
    one.send()
    first_part, last_part, *halves = mix_grads(
        place_all, bits_all, product_part, order(rim_back), mixer_all, low_all
    )
    order.mark(halves[1])
    rest = Scatter(order, *halves, bits_all)
    rest.send()
    two.add()
    two.send()
    three.add()
    three.send()
    rest.add()
    rest.send()
    input_grad = input_back(
        order(first_part), closing_low, last_part, weight_in, residual_grad, x, vec,
    )
    order.mark(input_grad)
    input_grad = input_grad.reshape(1, rows, features)
    two.add()
    two.send()
    three.add()
    three.send()
    outer.add()
    outer.send()
    rest.add()
    rest.send()
    three.add()
    three.send()
    layer_out = order.mark((residual + order(branch).astype(F32)).astype(BF16))
    layer_out = layer_out.reshape(1, rows, features)
    one.add()
    done = unpack(place, one.pieces, (), one.bits, wide, 0, features, hidden_units)
    order.mark(done[0])
    outer.add()
    outer.send()
    rest.add()
    rest.send()
    outer.add()
    outer.send()
    rest.add()
    rest.send()
    outer.finish()
    two.add()
    done = unpack(place, two.pieces, done, two.bits, wide, 1, features, hidden_units)
    order.mark(done[0])
    rest.finish()
    grad_out = outer.total[:, :features]
    grad_second = outer.total[:, features]
    grad_conv = outer.total[:, features + 1 : features + 1 + KERNEL]
    ends = rest.total
    grad_in = jnp.concatenate(
        [ends[:, :features], outer.total[:, features + LANES :], ends[:, features:]], 1
    )
    grad_first = jnp.sum(grad_in * in_proj.astype(F32), axis=1) / first_gain.astype(F32)
    three.add()
    grad_gate, grad_up, grad_down = unpack(
        place, three.pieces, done, three.bits, wide, 2, features, hidden_units
    )
    return (
        layer_out,
        input_grad,
        grad_first,
        grad_in,
        grad_conv,
        grad_out,
        grad_second,
        grad_gate,
        grad_up,
        grad_down,
    )


def solution(mesh):
    in_specs = (
        P("dp", "mp", None),
        P("dp", "mp"),
        P(("dp", "mp")),
        P(("dp", "mp"), None),
        P(("dp", "mp"), None),
        P(("dp", "mp"), None),
        P(("dp", "mp")),
        P(None, "mp"),
        P(None, "mp"),
        P("mp", None),
        P("dp", "mp", None),
    )
    out_specs = (
        P("dp", "mp", None),
        P("dp", "mp", None),
        P(("dp", "mp")),
        P(("dp", "mp"), None),
        P(("dp", "mp"), None),
        P(("dp", "mp"), None),
        P(("dp", "mp")),
        P(None, "mp"),
        P(None, "mp"),
        P("mp", None),
    )
    return jax.shard_map(
        per_device, mesh=mesh, in_specs=in_specs, out_specs=out_specs, check_vma=False
    )
```
